512 devices in a mesh: segment: 4 (over z_lo, core), expert: 16 (over z_hi, x), fsdp: 8 (over y).
Axes of the slice: x: 4, y: 8, z: 8 (z_hi: 4, z_lo: 2; z = z_hi * 2 + z_lo), core: 2. Of those that a mesh axis runs over, the one named last changes fastest.
Arguments:
- acts: bfloat16 [4, 2, 2048, 1024], P('segment', None, ('expert', 'fsdp')), may hold values from -6 to 6
- out_grad: bfloat16 [2, 2048, 1024], P(None, ('expert', 'fsdp')), may hold values from -6 to 6
- expert_ids: int32 [4, 2, 2048, 2], P('segment', None, ('expert', 'fsdp')), may hold values from 0 to 15, all different within a row; in each aligned block of 16 rows (0 to 15, 16 to 31, ..., all dimensions but the last counted through in order) at most 2 rows name the same one
- gates: bfloat16 [4, 2, 2048, 2], P('segment', None, ('expert', 'fsdp')), may hold values from 0.19921875 to 1
- w_gate: bfloat16 [4, 16, 1024, 2048], P('segment', 'expert', None, 'fsdp'), may hold values from -0.1875 to 0.1875
- w_up: bfloat16 [4, 16, 1024, 2048], P('segment', 'expert', None, 'fsdp'), may hold values from -0.1875 to 0.1875
- w_down: bfloat16 [4, 16, 2048, 1024], P('segment', 'expert', 'fsdp'), may hold values from -0.125 to 0.125
Outputs:
- act_grad: bfloat16 [4, 2, 2048, 1024], P('segment', None, ('expert', 'fsdp'))
- gate_grad: float32 [4, 2, 2048, 2], P('segment', None, ('expert', 'fsdp'))
- grad_w_gate: bfloat16 [4, 16, 1024, 2048], P('segment', 'expert', None, 'fsdp')
- grad_w_up: bfloat16 [4, 16, 1024, 2048], P('segment', 'expert', None, 'fsdp')
- grad_w_down: bfloat16 [4, 16, 2048, 1024], P('segment', 'expert', 'fsdp')
The draws below stay inside these ranges and needn't reach their ends.
Inputs may be any that keep to these rules, and one draw needn't show every extreme that they name: `expert_ids`: each row names 2 different experts. Within the tokens of one device for one layer and micro-batch (aligned blocks of 16 rows) no expert is named by more than 2 tokens, and in some such block an expert is named by exactly 2.
All inputs are finite; a program needn't handle non-finite values.
Results may differ from the reference program's by a relative error of at most 0.035.
Values may be sent and summed in bfloat16 or wider, within the bound.
No kernel may reach another device: no remote copies, remote signals or barrier semaphores. Data moves between devices by JAX's collectives and lax.ppermute only.
A program may use at most 64 MiB of HBM per device.

```python
import math
import jax
import jax.numpy as jnp
import numpy as np
from jax import lax

D = 1024
HID = 2048
TOP = 2
MB = 2
TOK_DEV = 16
SEGMENTS = 4
EXPERTS = 16
TOKENS = 2048
CAP = 2
N_EXPERT = 16
N_FSDP = 8


def block_levels(own_key, extent, cuts, least, largest):
    loudness = 1.0
    for dim, blocks in cuts:
        steps = jax.random.uniform(jax.random.fold_in(jax.random.fold_in(own_key, 6), dim), (blocks,), jnp.float32, least / len(cuts), largest / len(cuts))
        loudness = loudness * jnp.repeat(jnp.exp(steps), extent[dim] // blocks).reshape((-1,) + (1,) * (len(extent) - 1 - dim))
    return loudness


def shared_out(own_key, own, number, rows, amount, top, bound, skew):
    order = jax.random.permutation(own_key, amount)
    heavy_load, usual = shares(amount, rows * top, bound, skew, True), shares(amount, rows * top, bound, skew, False)
    places = jnp.arange(amount)

    def named(lengths, turn):
        used = int((lengths > 0).sum())
        fixed = max(1, used // 4)
        moved = fixed + (places - fixed + turn * (used - fixed)) % max(1, amount - fixed)
        return jnp.zeros((amount,), jnp.int32).at[order[jnp.where(places < fixed, places, moved)]].set(jnp.asarray(lengths, jnp.int32))

    lengths = jnp.where(number % 4 == 0, named(heavy_load, number // 4), named(usual, number - number // 4 - 1))
    mixed = jax.random.permutation(jax.random.fold_in(own, 3), amount)
    giver, taker = mixed[0:amount // 2 * 2:2], mixed[1:amount // 2 * 2:2]
    margin = jnp.minimum(lengths[giver] - 1, bound - lengths[taker]) // 2
    margin = jnp.where((giver == order[0]) | (taker == order[0]) | (lengths[taker] == 0), 0, jnp.maximum(margin, 0))
    moved = jax.random.randint(jax.random.fold_in(own, 4), (amount // 2,), 0, 1 << 20) % (margin + 1)
    lengths = lengths.at[giver].add(-moved).at[taker].add(moved)
    members = jnp.searchsorted(jnp.cumsum(lengths), jnp.arange(rows * top), side="right").astype(jnp.int32)
    table = members.reshape(top, rows).T
    table = table[jax.random.permutation(jax.random.fold_in(own, 1), rows)]
    turn = jax.random.randint(jax.random.fold_in(own, 2), (rows, 1), 0, top)
    return jnp.take_along_axis(table, (jnp.arange(top)[None, :] + turn) % top, axis=1)


def shares(number_of, total, bound, slope, full):
    weights = [(1 << 20) // math.isqrt(rank ** slope) + 1 for rank in range(1, number_of + 1)]
    largest = bound if full else min(bound, max(-(-total // number_of), total * weights[0] // sum(weights)))
    least = 1 if total - largest >= number_of - 1 else 0
    given, rest = [largest] + [least] * (number_of - 1), total - largest - least * (number_of - 1)
    while rest > 0:
        free = [i for i in range(1, number_of) if given[i] < largest] or [i for i in range(1, number_of) if given[i] < bound]
        mass, left = sum([weights[i] for i in free]), rest
        for i in free:
            addition = min(bound - given[i], max(1, left * weights[i] // mass), rest)
            given[i] = given[i] + addition
            rest = rest - addition
    return np.array(given)


def gaussian(rng, dims, width, reach, cuts=(), held_as=jnp.bfloat16):
    entries = jax.random.normal(rng, dims, jnp.float32) * width
    if len(cuts) > 0:
        entries = block_levels(rng, dims, cuts, -0.22, 0.18) * entries
    return jnp.clip(entries, min=-reach, max=reach).astype(held_as)


def setup_inputs(seed: int = 0) -> dict:
    key_of = jax.random.split(jax.random.key(seed), 8)
    acts = gaussian(key_of[0], (SEGMENTS, MB, TOKENS, D), 1.0, 6.0, ((0, 4), (2, 128)))
    out_grad = gaussian(key_of[1], (MB, TOKENS, D), 1.0, 6.0, ((1, 128),))
    expert_ids_keys = jax.random.split(jax.random.fold_in(key_of[2], 1), SEGMENTS * MB * TOKENS // TOK_DEV)
    expert_ids_turns = jax.random.permutation(jax.random.fold_in(key_of[2], 3), SEGMENTS * MB * TOKENS // TOK_DEV)
    expert_ids = jax.vmap(lambda own, number: shared_out(jax.random.fold_in(key_of[2], 2), own, number, TOK_DEV, EXPERTS, TOP, CAP, 2))(expert_ids_keys, expert_ids_turns).reshape((SEGMENTS, MB, TOKENS, TOP))
    gates = jnp.clip(0.19921875 + 0.80078125 * jax.random.uniform(key_of[3], (SEGMENTS, MB, TOKENS, TOP), jnp.float32) ** block_levels(key_of[3], (SEGMENTS, MB, TOKENS, TOP), ((0, 4), (2, 128)), -0.2, 0.2), 0.19921875, 1.0).astype(jnp.bfloat16)
    w_gate = gaussian(key_of[4], (SEGMENTS, EXPERTS, D, HID), D ** -0.5, 0.1875, ((0, 4), (1, 16), (3, 8)))
    w_up = gaussian(key_of[5], (SEGMENTS, EXPERTS, D, HID), D ** -0.5, 0.1875, ((0, 4), (1, 16), (3, 8)))
    w_down = gaussian(key_of[6], (SEGMENTS, EXPERTS, HID, D), HID ** -0.5, 0.125, ((0, 4), (1, 16), (2, 8)))
    return {"acts": acts, "out_grad": out_grad, "expert_ids": expert_ids, "gates": gates, "w_gate": w_gate, "w_up": w_up, "w_down": w_down}


def silu_parts(pre_gate):
    sigmoid = jax.nn.sigmoid(pre_gate)
    return pre_gate * sigmoid, sigmoid * (1.0 + pre_gate * (1.0 - sigmoid))


def expert_backward(packed):
    token_rows, grad_rows, gate_rows, w_first, w_third, w_second = packed
    pre_gate = jnp.dot(token_rows, w_first, preferred_element_type=jnp.float32)
    pre_up = jnp.dot(token_rows, w_third, preferred_element_type=jnp.float32)
    activated, slope_term = silu_parts(pre_gate)
    hidden = activated * pre_up
    back_hidden = jnp.dot(grad_rows, w_second.T, preferred_element_type=jnp.float32)
    gate_col = gate_rows.astype(jnp.float32)[:, None]
    scaled = back_hidden * gate_col
    grad_gate_pre = (scaled * pre_up * slope_term).astype(jnp.bfloat16)
    grad_up_pre = (scaled * activated).astype(jnp.bfloat16)
    hidden_gated = (hidden * gate_col).astype(jnp.bfloat16)
    grad_first = jnp.dot(token_rows.T, grad_gate_pre, preferred_element_type=jnp.float32)
    grad_third = jnp.dot(token_rows.T, grad_up_pre, preferred_element_type=jnp.float32)
    grad_second = jnp.dot(hidden_gated.T, grad_rows, preferred_element_type=jnp.float32)
    row_count = token_rows.shape[0]
    block_width = HID // N_FSDP
    part_rows = jnp.einsum('rch,dch->rcd', grad_gate_pre.astype(jnp.float32).reshape(row_count, N_FSDP, block_width), w_first.astype(jnp.float32).reshape(D, N_FSDP, block_width))
    part_rows = part_rows + jnp.einsum('rch,dch->rcd', grad_up_pre.astype(jnp.float32).reshape(row_count, N_FSDP, block_width), w_third.astype(jnp.float32).reshape(D, N_FSDP, block_width))
    part_rows = lax.optimization_barrier(part_rows.astype(jnp.bfloat16))
    row_grad = jnp.sum(part_rows.astype(jnp.float32), axis=1).astype(jnp.bfloat16)
    part_gates = jnp.sum((hidden * back_hidden).reshape(row_count, N_FSDP, block_width), axis=2)
    part_gates = lax.optimization_barrier(part_gates.astype(jnp.bfloat16))
    gate_sum = jnp.sum(part_gates.astype(jnp.float32), axis=1).astype(jnp.bfloat16)
    return row_grad, gate_sum, grad_first, grad_third, grad_second


def layer_backward(acts_in, grad_in, ids_in, gates_in, w_first_all, w_third_all, w_second_all):
    sources = N_EXPERT * N_FSDP
    ids_block = ids_in.reshape(sources, TOK_DEV, TOP).astype(jnp.int32)
    table = (ids_block[..., None] == jnp.arange(EXPERTS, dtype=jnp.int32)).astype(jnp.int32)
    counts = jnp.sum(table, axis=2)
    before = jnp.cumsum(counts, axis=1) - counts
    slots = jnp.sum(before[:, :, None, :] * table, axis=3)
    source_ids = jnp.arange(sources, dtype=jnp.int32)[:, None, None]
    target = ((ids_block * sources + source_ids) * CAP + slots).reshape(-1).astype(jnp.int32)
    total = EXPERTS * sources * CAP
    spread_acts = jnp.broadcast_to(acts_in[:, None, :], (TOKENS, TOP, D)).reshape(-1, D)
    spread_grads = jnp.broadcast_to(grad_in[:, None, :], (TOKENS, TOP, D)).reshape(-1, D)
    token_buf = jnp.zeros((total, D), jnp.bfloat16).at[target].set(spread_acts)
    grad_buf = jnp.zeros((total, D), jnp.bfloat16).at[target].set(spread_grads)
    gate_buf = jnp.zeros((total,), jnp.bfloat16).at[target].set(gates_in.reshape(-1))
    per_expert = sources * CAP
    outputs = lax.map(expert_backward, (token_buf.reshape(EXPERTS, per_expert, D), grad_buf.reshape(EXPERTS, per_expert, D), gate_buf.reshape(EXPERTS, per_expert), w_first_all, w_third_all, w_second_all))
    row_grads, gate_sums, grad_first, grad_third, grad_second = outputs
    returned = row_grads.reshape(total, D)[target].reshape(TOKENS, TOP, D).astype(jnp.float32)
    new_grad = (grad_in.astype(jnp.float32) + jnp.sum(returned, axis=1)).astype(jnp.bfloat16)
    gate_back = gate_sums.reshape(total)[target].reshape(TOKENS, TOP).astype(jnp.float32)
    return new_grad, gate_back, grad_first, grad_third, grad_second


def reference(acts, out_grad, expert_ids, gates, w_gate, w_up, w_down):
    act_out = jnp.zeros((SEGMENTS, MB, TOKENS, D), jnp.bfloat16)
    gate_out = jnp.zeros((SEGMENTS, MB, TOKENS, TOP), jnp.float32)
    sum_first = jnp.zeros((SEGMENTS, EXPERTS, D, HID), jnp.float32)
    sum_third = jnp.zeros((SEGMENTS, EXPERTS, D, HID), jnp.float32)
    sum_second = jnp.zeros((SEGMENTS, EXPERTS, HID, D), jnp.float32)
    for micro_index in range(MB):
        incoming = out_grad[micro_index]
        for segment_index in reversed(range(SEGMENTS)):
            result = layer_backward(acts[segment_index, micro_index], incoming, expert_ids[segment_index, micro_index], gates[segment_index, micro_index], w_gate[segment_index], w_up[segment_index], w_down[segment_index])
            act_out = act_out.at[segment_index, micro_index].set(result[0])
            gate_out = gate_out.at[segment_index, micro_index].set(result[1])
            sum_first = sum_first.at[segment_index].add(result[2])
            sum_third = sum_third.at[segment_index].add(result[3])
            sum_second = sum_second.at[segment_index].add(result[4])
            incoming = result[0]
    return act_out, gate_out, sum_first.astype(jnp.bfloat16), sum_third.astype(jnp.bfloat16), sum_second.astype(jnp.bfloat16)
```

```python
import jax
import jax.numpy as jnp
from jax import lax
from jax.experimental import pallas as pl
from jax.experimental.pallas import tpu as pltpu
from jax.sharding import PartitionSpec as P

BF = jnp.bfloat16
F32 = jnp.float32
NN = (((1,), (0,)), ((), ()))
NT = (((1,), (1,)), ((), ()))
TN = (((0,), (0,)), ((), ()))
LANES = 128
ROUTE = ("expert", "fsdp")


def dot(a, b, dims):
    return lax.dot_general(a, b, dims, preferred_element_type=F32)


def iota(shape, dim):
    return lax.broadcasted_iota(jnp.int32, shape, dim)


def call(body, outs, *args):
    return pl.pallas_call(
        body,
        out_shape=[jax.ShapeDtypeStruct(s, d) for s, d in outs],
        in_specs=[pl.BlockSpec(memory_space=pltpu.VMEM)] * len(args),
        out_specs=[pl.BlockSpec(memory_space=pltpu.VMEM)] * len(outs),
        compiler_params=pltpu.CompilerParams(vmem_limit_bytes=48 * 1024 * 1024),
    )(*args)


def upper(rows, cols):
    return (iota((rows, cols), 0) % 8) >= 4


def place(routing, tokens):
    half = tokens.shape[1] // 2
    spread = dot(routing, tokens, TN)
    rows = spread.shape[0]
    return jnp.where(upper(rows, half), spread[:, half:], spread[:, :half]).astype(BF)


def prep_body(micro, tok, cap, n_expert, n_fsdp, ids_ref, gates_ref, x_ref, send_ref, put_ref, get_ref, getz_ref):
    rows = micro * tok
    ids = ids_ref[...]
    gates = gates_ref[...]
    first, second = ids[:, 0:1], ids[:, 1:2]
    experts = iota((rows, LANES), 1)
    one, two = experts == first, experts == second
    counts = (one | two).astype(BF)
    r0, r1 = iota((rows, rows), 0), iota((rows, rows), 1)
    lower = ((r1 < r0) & (r1 // tok == r0 // tok)).astype(BF)
    before = dot(lower, counts, NN)
    place_of = iota((rows, 1), 0) // tok * cap
    slot_one = jnp.sum(jnp.where(one, before, 0.0), axis=1, keepdims=True).astype(jnp.int32) + place_of
    slot_two = jnp.sum(jnp.where(two, before, 0.0), axis=1, keepdims=True).astype(jnp.int32) + place_of
    cols = 8 * n_expert
    col = iota((rows, cols), 1)
    put_one = ((col // 8 == first) & (col % 4 == slot_one)).astype(F32)
    put_two = ((col // 8 == second) & (col % 4 == slot_two)).astype(F32)
    put = (put_one + put_two).astype(BF)
    put_ref[...] = put
    put_gates = (put_one * gates[:, 0:1] + put_two * gates[:, 1:2]).astype(BF)
    gate_cols = dot(put_gates, jnp.ones((rows, LANES), BF), TN).astype(BF)
    spread = jnp.concatenate([place(put, x_ref[...]), gate_cols], axis=1)
    width = spread.shape[1]
    send_ref[...] = jnp.broadcast_to(spread.reshape(n_expert, 1, 8, width), (n_expert, n_fsdp, 8, width))
    total = 8 * n_expert * n_fsdp
    wide = iota((rows, total), 1)
    target = wide // (8 * n_fsdp)
    row = wide % 4
    low = (wide % 8) < 4
    hit_one = (target == first) & (row == slot_one)
    hit_two = (target == second) & (row == slot_two)
    hit = hit_one | hit_two
    get_ref[:rows] = jnp.where(hit & low, 1.0, 0.0).astype(BF)
    get_ref[rows:] = jnp.where(hit & ~low, 1.0, 0.0).astype(BF)
    getz_ref[:rows] = jnp.where(hit_one & low, 1.0, 0.0).astype(BF)
    getz_ref[rows:] = jnp.where(hit_two & low, 1.0, 0.0).astype(BF)


def place_body(n_expert, n_fsdp, put_ref, g_ref, send_ref):
    spread = place(put_ref[...], g_ref[...])
    width = spread.shape[1]
    send_ref[...] = jnp.broadcast_to(spread.reshape(n_expert, 1, 8, width), (n_expert, n_fsdp, 8, width))


def join(mine, other, mask):
    value = jnp.where(mask, other, mine)
    rows, cols = value.shape
    turned = pltpu.roll(value.reshape(rows // 8, 8, cols), 4, 1).reshape(rows, cols)
    return value + turned


CHUNK = 256


def forward_body(rows_ref, wg_ref, wu_ref, slope_ref, act_ref, hid_ref, hg_ref):
    total = rows_ref.shape[0]
    half = wg_ref.shape[0] // 2

    def step(i, carry):
        at = pl.ds(pl.multiple_of(i * CHUNK, CHUNK), CHUNK)
        x = rows_ref[at, :half]
        c = rows_ref[at, half:].astype(F32)
        c = jnp.concatenate([c] * (wg_ref.shape[1] // LANES), axis=1)
        mask = upper(CHUNK, wg_ref.shape[1])
        a = join(dot(x, wg_ref[:half, :], NN), dot(x, wg_ref[half:, :], NN), mask)
        b = join(dot(x, wu_ref[:half, :], NN), dot(x, wu_ref[half:, :], NN), mask)
        sig = jax.nn.sigmoid(a)
        s = a * sig
        slope_ref[at, :] = c * (b * (sig * (1.0 + a * (1.0 - sig))))
        act_ref[at, :] = c * s
        h = s * b
        hid_ref[at, :] = h
        hg_ref[at, :] = (c * h).astype(BF)
        return carry

    lax.fori_loop(0, total // CHUNK, step, 0)


def back_body(rows_ref, wd_ref, wg_ref, wu_ref, slope_ref, act_ref, hid_ref, out_ref, da_ref, db_ref):
    total = rows_ref.shape[0]
    half = wg_ref.shape[0] // 2

    def step(i, carry):
        at = pl.ds(pl.multiple_of(i * CHUNK, CHUNK), CHUNK)
        g = rows_ref[at, :]
        mask = upper(CHUNK, wd_ref.shape[0])
        q = join(dot(g, wd_ref[:, :half], NT), dot(g, wd_ref[:, half:], NT), mask)
        da = (q * slope_ref[at, :]).astype(BF)
        db = (q * act_ref[at, :]).astype(BF)
        da_ref[at, :] = da
        db_ref[at, :] = db
        low = dot(da, wg_ref[:half, :], NT) + dot(db, wu_ref[:half, :], NT)
        high = dot(da, wg_ref[half:, :], NT) + dot(db, wu_ref[half:, :], NT)
        out_ref[at, :half] = jnp.where(upper(CHUNK, half), high, low).astype(BF)
        z = jnp.sum(q * hid_ref[at, :], axis=1, keepdims=True)
        out_ref[at, half:] = jnp.broadcast_to(z, (CHUNK, LANES)).astype(BF)
        return carry

    lax.fori_loop(0, total // CHUNK, step, 0)


def merge_body(get_ref, getz_ref, back_ref, g_ref, new_ref, gate_ref):
    tokens, width = g_ref.shape
    half = width // 2
    summed = dot(get_ref[...], back_ref[:, :half], NN)
    g = g_ref[...].astype(F32)
    new_ref[:, :half] = (g[:, :half] + summed[:tokens]).astype(BF)
    new_ref[:, half:] = (g[:, half:] + summed[tokens:]).astype(BF)
    gate_ref[...] = dot(getz_ref[...], back_ref[:, half:], NN)


def local(acts, out_grad, expert_ids, gates, w_gate, w_up, w_down):
    segments = lax.axis_size("segment")
    segment = lax.axis_index("segment")
    n_expert = lax.axis_size("expert")
    n_fsdp = lax.axis_size("fsdp")
    _, micro, tok, width = acts.shape
    top = expert_ids.shape[3]
    cap = top * tok // n_expert
    tokens = micro * tok
    half = width // 2
    wide = half + LANES
    wg, wu, wd = w_gate[0, 0], w_up[0, 0], w_down[0, 0]
    hid = wg.shape[1]
    total = 8 * n_expert * n_fsdp
    sources = n_expert * n_fsdp

    def exchange(value):
        cols = value.shape[-1]
        moved = lax.all_to_all(value.reshape(sources, 8, cols), ROUTE, 0, 0, tiled=True)
        return moved.reshape(total, cols)

    send, put, get, getz = call(
        lambda *r: prep_body(micro, tok, cap, n_expert, n_fsdp, *r),
        [((n_expert, n_fsdp, 8, wide), BF), ((tokens, 8 * n_expert), BF), ((2 * tokens, total), BF), ((top * tokens, total), BF)],
        expert_ids.reshape(tokens, top),
        gates.reshape(tokens, top).astype(F32),
        acts.reshape(tokens, width),
    )
    x_rows = exchange(send)
    slope, act, hidden, hg = call(
        forward_body,
        [((total, hid), F32), ((total, hid), F32), ((total, hid), F32), ((total, hid), BF)],
        x_rows, wg, wu,
    )

    def run(grad):
        (send_g,) = call(
            lambda *r: place_body(n_expert, n_fsdp, *r), [((n_expert, n_fsdp, 8, half), BF)], put, grad
        )
        g_rows = exchange(send_g)
        out, da, db = call(
            back_body,
            [((total, wide), BF), ((total, hid), BF), ((total, hid), BF)],
            g_rows, wd, wg, wu, slope, act, hidden,
        )
        back = exchange(out)
        new, gate_new = call(
            merge_body, [((tokens, width), BF), ((top * tokens, LANES), F32)], get, getz, back, grad
        )
        return new, gate_new, g_rows, da, db

    state = (
        jnp.zeros((tokens, width), BF),
        jnp.zeros((top * tokens, LANES), F32),
        jnp.zeros((total, half), BF),
        jnp.zeros((total, hid), BF),
        jnp.zeros((total, hid), BF),
    )
    grad = out_grad.reshape(tokens, width)
    for layer in reversed(range(segments)):
        state = lax.cond(segment == layer, lambda g, s: tuple(run(g)), lambda g, s: s, grad, state)
        if layer > 0:
            grad = lax.ppermute(state[0], "segment", [(layer, layer - 1)])
    new, gate_new, g_rows, da, db = state

    lower = (iota((total, hid), 0) % 8) < 4
    zero = jnp.zeros((), BF)

    def halves(value):
        return jnp.concatenate([jnp.where(lower, value, zero), jnp.where(lower, zero, value)], axis=1)

    def outer(value):
        both = dot(x_rows[:, :half], halves(value), TN)
        return jnp.concatenate([both[:, :hid], both[:, hid:]], axis=0).astype(BF)[None, None]

    grad_gate = outer(da)
    grad_up = outer(db)
    both = dot(halves(hg), g_rows, TN)
    grad_down = jnp.concatenate([both[:hid], both[hid:]], axis=1).astype(BF)[None, None]
    gate_out = gate_new[:, 0].reshape(top, micro, tok).transpose(1, 2, 0)[None]
    return new.reshape(acts.shape), gate_out, grad_gate, grad_up, grad_down


def solution(mesh):
    in_specs = (
        P("segment", None, ("expert", "fsdp"), None),
        P(None, ("expert", "fsdp"), None),
        P("segment", None, ("expert", "fsdp"), None),
        P("segment", None, ("expert", "fsdp"), None),
        P("segment", "expert", None, "fsdp"),
        P("segment", "expert", None, "fsdp"),
        P("segment", "expert", "fsdp", None),
    )
    out_specs = (
        P("segment", None, ("expert", "fsdp"), None),
        P("segment", None, ("expert", "fsdp"), None),
        P("segment", "expert", None, "fsdp"),
        P("segment", "expert", None, "fsdp"),
        P("segment", "expert", "fsdp", None),
    )
    return jax.shard_map(local, mesh=mesh, in_specs=in_specs, out_specs=out_specs, check_vma=False)
```

```python
import jax
import jax.numpy as jnp
from jax import lax
from jax.experimental import pallas as pl
from jax.experimental.pallas import tpu as pltpu
from jax.sharding import PartitionSpec as P

BF = jnp.bfloat16
F32 = jnp.float32
NN = (((1,), (0,)), ((), ()))
NT = (((1,), (1,)), ((), ()))
TN = (((0,), (0,)), ((), ()))
LANES = 128
CHUNK = 256
ROUTE = ("expert", "fsdp")


def dot(a, b, dims):
    return lax.dot_general(a, b, dims, preferred_element_type=F32)


def iota(shape, dim):
    return lax.broadcasted_iota(jnp.int32, shape, dim)


def call(body, outs, *args, cost=None):
    return pl.pallas_call(
        body,
        out_shape=[jax.ShapeDtypeStruct(s, d) for s, d in outs],
        in_specs=[pl.BlockSpec(memory_space=pltpu.VMEM)] * len(args),
        out_specs=[pl.BlockSpec(memory_space=pltpu.VMEM)] * len(outs),
        compiler_params=pltpu.CompilerParams(vmem_limit_bytes=48 * 1024 * 1024),
        cost_estimate=cost,
    )(*args)


def call_rows(body, outs, streamed, whole):
    total = streamed[0].shape[0]
    by_rows = lambda shape: pl.BlockSpec((CHUNK, shape[1]), lambda i: (i, 0))
    return pl.pallas_call(
        body,
        grid=(total // CHUNK,),
        out_shape=[jax.ShapeDtypeStruct(s, d) for s, d in outs],
        in_specs=[by_rows(v.shape) for v in streamed] + [pl.BlockSpec(memory_space=pltpu.VMEM)] * len(whole),
        out_specs=[by_rows(s) for s, _ in outs],
        compiler_params=pltpu.CompilerParams(vmem_limit_bytes=48 * 1024 * 1024),
    )(*streamed, *whole)


def upper(rows, cols):
    return (iota((rows, cols), 0) % 8) >= 4


def place(routing, tokens):
    half = tokens.shape[1] // 2
    spread = dot(routing, tokens, TN)
    rows = spread.shape[0]
    return jnp.where(upper(rows, half), spread[:, half:], spread[:, :half]).astype(BF)


def prep_body(micro, tok, cap, n_expert, n_fsdp, ids_ref, gates_ref, x_ref, spread_ref, put_ref, get_ref, getz_ref):
    rows = micro * tok
    ids = jnp.concatenate([ids_ref[0, m] for m in range(micro)], axis=0)
    gates = jnp.concatenate([gates_ref[0, m].astype(F32) for m in range(micro)], axis=0)
    first, second = ids[:, 0:1], ids[:, 1:2]
    experts = iota((rows, LANES), 1)
    one, two = experts == first, experts == second
    counts = (one | two).astype(BF)
    r0, r1 = iota((rows, rows), 0), iota((rows, rows), 1)
    lower = ((r1 < r0) & (r1 // tok == r0 // tok)).astype(BF)
    before = dot(lower, counts, NN)
    place_of = iota((rows, 1), 0) // tok * cap
    slot_one = jnp.sum(jnp.where(one, before, 0.0), axis=1, keepdims=True).astype(jnp.int32) + place_of
    slot_two = jnp.sum(jnp.where(two, before, 0.0), axis=1, keepdims=True).astype(jnp.int32) + place_of
    cols = 8 * n_expert
    col = iota((rows, cols), 1)
    put_one = ((col // 8 == first) & (col % 4 == slot_one)).astype(F32)
    put_two = ((col // 8 == second) & (col % 4 == slot_two)).astype(F32)
    put = (put_one + put_two).astype(BF)
    put_ref[...] = put
    put_gates = (put_one * gates[:, 0:1] + put_two * gates[:, 1:2]).astype(BF)
    half = x_ref.shape[1] // 2
    spread_ref[:, :half] = place(put, x_ref[...])
    spread_ref[:, half:] = dot(put_gates, jnp.ones((rows, LANES), BF), TN).astype(BF)
    total = 8 * n_expert * n_fsdp
    wide = iota((rows, total), 1)
    target = wide // (8 * n_fsdp)
    row = wide % 4
    low = (wide % 8) < 4
    hit_one = (target == first) & (row == slot_one)
    hit_two = (target == second) & (row == slot_two)
    hit = hit_one | hit_two
    get_ref[:rows] = jnp.where(hit & low, 1.0, 0.0).astype(BF)
    get_ref[rows:] = jnp.where(hit & ~low, 1.0, 0.0).astype(BF)
    getz_ref[:rows] = jnp.where(hit_one & low, 1.0, 0.0).astype(BF)
    getz_ref[rows:] = jnp.where(hit_two & low, 1.0, 0.0).astype(BF)


def fan(send_ref, value, at):
    n_expert, n_fsdp = send_ref.shape[:2]
    width = value.shape[1]
    send_ref[:, :, :, at : at + width] = jnp.broadcast_to(
        value.reshape(n_expert, 1, 8, width), (n_expert, n_fsdp, 8, width)
    )


def place_body(put_ref, g_ref, send_ref):
    fan(send_ref, place(put_ref[...], g_ref[...]), 0)


def fan_body(spread_ref, send_ref):
    fan(send_ref, spread_ref[...], 0)


def place_both_body(spread_ref, put_ref, g_ref, send_ref):
    fan(send_ref, spread_ref[...], 0)
    fan(send_ref, place(put_ref[...], g_ref[...]), spread_ref.shape[1])


def join(mine, other, mask):
    value = jnp.where(mask, other, mine)
    rows, cols = value.shape
    turned = pltpu.roll(value.reshape(rows // 8, 8, cols), 4, 1).reshape(rows, cols)
    return value + turned


def forward(x, c, wg_ref, wu_ref):
    half, hid = wg_ref.shape[0] // 2, wg_ref.shape[1]
    c = jnp.concatenate([c.astype(F32)] * (hid // LANES), axis=1)
    mask = upper(x.shape[0], hid)
    a = join(dot(x, wg_ref[:half, :], NN), dot(x, wg_ref[half:, :], NN), mask)
    b = join(dot(x, wu_ref[:half, :], NN), dot(x, wu_ref[half:, :], NN), mask)
    sig = jax.nn.sigmoid(a)
    s = a * sig
    h = s * b
    return c * (b * (sig * (1.0 + a * (1.0 - sig)))), c * s, h, (c * h).astype(BF)


def backward(g, slope, act, hidden, wd_ref, wg_ref, wu_ref):
    half, hid = wg_ref.shape[0] // 2, wg_ref.shape[1]
    rows = g.shape[0]
    q = join(dot(g, wd_ref[:, :half], NT), dot(g, wd_ref[:, half:], NT), upper(rows, hid))
    da = (q * slope).astype(BF)
    db = (q * act).astype(BF)
    low = dot(da, wg_ref[:half, :], NT) + dot(db, wu_ref[:half, :], NT)
    high = dot(da, wg_ref[half:, :], NT) + dot(db, wu_ref[half:, :], NT)
    out = jnp.where(upper(rows, half), high, low).astype(BF)
    z = jnp.sum(q * hidden, axis=1, keepdims=True)
    return da, db, out, jnp.broadcast_to(z, (rows, LANES)).astype(BF)


def forward_body(rows_ref, wg_ref, wu_ref, slope_ref, act_ref, hid_ref, hg_ref, x_ref):
    half = wg_ref.shape[0] // 2
    x = rows_ref[:, :half]
    x_ref[...] = x
    slope, act, hidden, hg_ref[...] = forward(x, rows_ref[:, half:], wg_ref, wu_ref)
    slope_ref[...] = slope.astype(BF)
    act_ref[...] = act.astype(BF)
    hid_ref[...] = hidden.astype(BF)


def back_body(rows_ref, slope_ref, act_ref, hid_ref, wd_ref, wg_ref, wu_ref, out_ref, da_ref, db_ref, *z_ref):
    half = wg_ref.shape[0] // 2
    da_ref[...], db_ref[...], out, z = backward(
        rows_ref[...],
        slope_ref[...].astype(F32),
        act_ref[...].astype(F32),
        hid_ref[...].astype(F32),
        wd_ref,
        wg_ref,
        wu_ref,
    )
    out_ref[:, :half] = out
    if z_ref:
        z_ref[0][...] = z
    else:
        out_ref[:, half:] = z


def both_body(rows_ref, wd_ref, wg_ref, wu_ref, out_ref, da_ref, db_ref, z_ref, hg_ref, x_ref, g_ref):
    half = wg_ref.shape[0] // 2
    x = rows_ref[:, :half]
    g = rows_ref[:, half + LANES :]
    x_ref[...] = x
    g_ref[...] = g
    slope, act, hidden, hg_ref[...] = forward(x, rows_ref[:, half : half + LANES], wg_ref, wu_ref)
    da_ref[...], db_ref[...], out_ref[...], z_ref[...] = backward(g, slope, act, hidden, wd_ref, wg_ref, wu_ref)


def merge_body(get_ref, back_ref, g_ref, new_ref):
    tokens, width = g_ref.shape
    half = width // 2
    summed = dot(get_ref[...], back_ref[:, :half], NN)
    g = g_ref[...].astype(F32)
    new_ref[:, :half] = (g[:, :half] + summed[:tokens]).astype(BF)
    new_ref[:, half:] = (g[:, half:] + summed[tokens:]).astype(BF)


def gate_body(getz_ref, z_ref, gate_ref):
    _, micro, tok, top = gate_ref.shape
    value = dot(getz_ref[...], z_ref[:, z_ref.shape[1] - LANES :], NN)
    for m in range(micro):
        parts = [value[(k * micro + m) * tok : (k * micro + m + 1) * tok, 0:1] for k in range(top)]
        gate_ref[0, m] = jnp.concatenate(parts, axis=1)


def outer_body(x_ref, g_ref, da_ref, db_ref, hg_ref, gate_ref, up_ref, down_ref):
    total, half = x_ref.shape
    hid = da_ref.shape[1]
    mask = upper(total, hid)
    x = x_ref[...]
    for k in range(2):
        at = slice(k * half, (k + 1) * half)
        keep = mask if k else ~mask
        only = lambda ref: jnp.where(keep, ref[...].astype(F32), 0.0).astype(BF)
        gate_ref[0, 0, at, :] = dot(x, only(da_ref), TN).astype(BF)
        up_ref[0, 0, at, :] = dot(x, only(db_ref), TN).astype(BF)
        down_ref[0, 0, :, at] = dot(only(hg_ref), g_ref[...], TN).astype(BF)


def local(acts, out_grad, expert_ids, gates, w_gate, w_up, w_down):
    segments = lax.axis_size("segment")
    segment = lax.axis_index("segment")
    n_expert = lax.axis_size("expert")
    n_fsdp = lax.axis_size("fsdp")
    _, micro, tok, width = acts.shape
    top = expert_ids.shape[3]
    cap = top * tok // n_expert
    tokens = micro * tok
    half = width // 2
    wide = half + LANES
    wg, wu, wd = w_gate[0, 0], w_up[0, 0], w_down[0, 0]
    hid = wg.shape[1]
    total = 8 * n_expert * n_fsdp
    sources = n_expert * n_fsdp
    last = segments - 1

    def exchange(value):
        cols = value.shape[-1]
        moved = lax.all_to_all(value.reshape(sources, 8, cols), ROUTE, 0, 0, tiled=True)
        return moved.reshape(total, cols)

    def rows_of(*cols):
        return [((total, c), BF) for c in cols]

    spread, put, get, getz = call(
        lambda *r: prep_body(micro, tok, cap, n_expert, n_fsdp, *r),
        [((8 * n_expert, wide), BF), ((tokens, 8 * n_expert), BF), ((2 * tokens, total), BF), ((top * tokens, total), BF)],
        expert_ids,
        gates,
        acts.reshape(tokens, width),
    )
    loss_grad = out_grad.reshape(tokens, width)

    def merge(back, grad):
        return call(merge_body, [((tokens, width), BF)], get, back, grad)[0]

    def gate_of(value):
        return call(gate_body, [((1, micro, tok, top), F32)], getz, value)[0]

    def outer(x_rows, g_rows, da, db, hg):
        cost = pl.CostEstimate(flops=12 * total * width * hid, bytes_accessed=12 * total * half, transcendentals=0)
        shapes = [(w_gate.shape, BF), (w_up.shape, BF), (w_down.shape, BF)]
        return tuple(call(outer_body, shapes, x_rows, g_rows, da, db, hg, cost=cost))

    def first():
        (send,) = call(
            place_both_body, [((n_expert, n_fsdp, 8, wide + half), BF)], spread, put, loss_grad
        )
        rows = exchange(send)
        out, da, db, z, hg, x_rows, g_rows = call_rows(
            both_body, rows_of(half, hid, hid, LANES, hid, half, half), [rows], [wd, wg, wu]
        )
        new = merge(exchange(out), loss_grad)
        unused = jnp.zeros((total, hid), BF)
        return (new, z, g_rows, da, db), (x_rows, unused, unused, unused, hg)

    def gather_rows():
        (send,) = call(fan_body, [((n_expert, n_fsdp, 8, wide), BF)], spread)
        early = lax.cond(segment == last - 1, exchange, lambda v: v.reshape(total, wide), send)
        token = 1.0 + 0.0 * early[0, :8].astype(F32)
        go = sum(lax.ppermute(token, "segment", [(last - 1, k)]) for k in range(last - 1))
        rows = lax.cond(
            go[0] > 0.5, lambda v, e: exchange(v), lambda v, e: e, send, early
        )
        slope, act, hidden, hg, x_rows = call_rows(
            forward_body, rows_of(hid, hid, hid, hid, half), [rows], [wg, wu]
        )
        state = (
            jnp.zeros((tokens, width), BF),
            jnp.zeros((total, LANES), BF),
            jnp.zeros((total, half), BF),
            jnp.zeros((total, hid), BF),
            jnp.zeros((total, hid), BF),
        )
        return state, (x_rows, slope, act, hidden, hg)

    state, saved = lax.cond(segment == last, first, gather_rows)
    x_rows, slope, act, hidden, hg = saved

    def dispatch(grad):
        (send,) = call(place_body, [((n_expert, n_fsdp, 8, half), BF)], put, grad)
        return exchange(send)

    def middle(grad, state):
        g_rows = dispatch(grad)
        out, da, db, z = call_rows(
            back_body, rows_of(half, hid, hid, LANES), [g_rows, slope, act, hidden], [wd, wg, wu]
        )
        new = merge(exchange(out), grad)
        return new, z, g_rows, da, db

    def final(grad, state):
        g_rows = dispatch(grad)
        out, da, db = call_rows(
            back_body, rows_of(wide, hid, hid), [g_rows, slope, act, hidden], [wd, wg, wu]
        )
        back = exchange(out)
        grads = outer(x_rows, g_rows, da, db, hg)
        return (merge(back, grad), gate_of(back)) + grads

    def finish(grad, state):
        new, z, g_rows, da, db = state
        return (new, gate_of(exchange(z))) + outer(x_rows, g_rows, da, db, hg)

    def step_down(layer, new):
        return lax.ppermute(new, "segment", [(layer, layer - 1)])

    grad = step_down(last, state[0])
    for layer in range(last - 1, 0, -1):
        state = lax.cond(segment == layer, middle, lambda g, s: s, grad, state)
        grad = step_down(layer, state[0])
    new, gate, grad_gate, grad_up, grad_down = lax.cond(segment == 0, final, finish, grad, state)
    return new.reshape(acts.shape), gate, grad_gate, grad_up, grad_down


def solution(mesh):
    in_specs = (
        P("segment", None, ("expert", "fsdp"), None),
        P(None, ("expert", "fsdp"), None),
        P("segment", None, ("expert", "fsdp"), None),
        P("segment", None, ("expert", "fsdp"), None),
        P("segment", "expert", None, "fsdp"),
        P("segment", "expert", None, "fsdp"),
        P("segment", "expert", "fsdp", None),
    )
    out_specs = (
        P("segment", None, ("expert", "fsdp"), None),
        P("segment", None, ("expert", "fsdp"), None),
        P("segment", "expert", None, "fsdp"),
        P("segment", "expert", None, "fsdp"),
        P("segment", "expert", "fsdp", None),
    )
    return jax.shard_map(local, mesh=mesh, in_specs=in_specs, out_specs=out_specs, check_vma=False)
```

```python
import jax
import jax.numpy as jnp
from jax import lax
from jax.experimental import pallas as pl
from jax.experimental.pallas import tpu as pltpu
from jax.sharding import PartitionSpec as P

BF = jnp.bfloat16
F32 = jnp.float32
NN = (((1,), (0,)), ((), ()))
NT = (((1,), (1,)), ((), ()))
TN = (((0,), (0,)), ((), ()))
LANES = 128
CHUNK = 512
ROUTE = ("expert", "fsdp")


def dot(a, b, dims):
    return lax.dot_general(a, b, dims, preferred_element_type=F32)


def iota(shape, dim):
    return lax.broadcasted_iota(jnp.int32, shape, dim)


def call(body, outs, *args, cost=None):
    return pl.pallas_call(
        body,
        out_shape=[jax.ShapeDtypeStruct(s, d) for s, d in outs],
        in_specs=[pl.BlockSpec(memory_space=pltpu.VMEM)] * len(args),
        out_specs=[pl.BlockSpec(memory_space=pltpu.VMEM)] * len(outs),
        compiler_params=pltpu.CompilerParams(vmem_limit_bytes=48 * 1024 * 1024),
        cost_estimate=cost,
    )(*args)


def call_rows(body, outs, streamed, whole):
    total = streamed[0].shape[0]
    by_rows = lambda shape: pl.BlockSpec((CHUNK, shape[1]), lambda i: (i, 0))
    return pl.pallas_call(
        body,
        grid=(total // CHUNK,),
        out_shape=[jax.ShapeDtypeStruct(s, d) for s, d in outs],
        in_specs=[by_rows(v.shape) for v in streamed] + [pl.BlockSpec(memory_space=pltpu.VMEM)] * len(whole),
        out_specs=[by_rows(s) for s, _ in outs],
        compiler_params=pltpu.CompilerParams(vmem_limit_bytes=48 * 1024 * 1024),
    )(*streamed, *whole)


def upper(rows, cols):
    return (iota((rows, cols), 0) % 8) >= 4


def place(routing, tokens):
    half = tokens.shape[1] // 2
    spread = dot(routing, tokens, TN)
    rows = spread.shape[0]
    return jnp.where(upper(rows, half), spread[:, half:], spread[:, :half]).astype(BF)


def prep_body(micro, tok, cap, n_expert, n_fsdp, ids_ref, gates_ref, x_ref, spread_ref, put_ref, get_ref, getz_ref):
    rows = micro * tok
    ids = jnp.concatenate([ids_ref[0, m] for m in range(micro)], axis=0)
    gates = jnp.concatenate([gates_ref[0, m].astype(F32) for m in range(micro)], axis=0)
    first, second = ids[:, 0:1], ids[:, 1:2]
    experts = iota((rows, LANES), 1)
    one, two = experts == first, experts == second
    counts = (one | two).astype(BF)
    r0, r1 = iota((rows, rows), 0), iota((rows, rows), 1)
    lower = ((r1 < r0) & (r1 // tok == r0 // tok)).astype(BF)
    before = dot(lower, counts, NN)
    place_of = iota((rows, 1), 0) // tok * cap
    slot_one = jnp.sum(jnp.where(one, before, 0.0), axis=1, keepdims=True).astype(jnp.int32) + place_of
    slot_two = jnp.sum(jnp.where(two, before, 0.0), axis=1, keepdims=True).astype(jnp.int32) + place_of
    cols = 8 * n_expert
    col = iota((rows, cols), 1)
    put_one = ((col // 8 == first) & (col % 4 == slot_one)).astype(F32)
    put_two = ((col // 8 == second) & (col % 4 == slot_two)).astype(F32)
    put = (put_one + put_two).astype(BF)
    put_ref[...] = put
    put_gates = (put_one * gates[:, 0:1] + put_two * gates[:, 1:2]).astype(BF)
    half = x_ref.shape[1] // 2
    spread_ref[:, :half] = place(put, x_ref[...])
    spread_ref[:, half:] = dot(put_gates, jnp.ones((rows, LANES), BF), TN).astype(BF)
    total = 8 * n_expert * n_fsdp
    wide = iota((rows, total), 1)
    target = wide // (8 * n_fsdp)
    row = wide % 4
    low = (wide % 8) < 4
    hit_one = (target == first) & (row == slot_one)
    hit_two = (target == second) & (row == slot_two)
    hit = hit_one | hit_two
    get_ref[:rows] = jnp.where(hit & low, 1.0, 0.0).astype(BF)
    get_ref[rows:] = jnp.where(hit & ~low, 1.0, 0.0).astype(BF)
    getz_ref[:rows] = jnp.where(hit_one & low, 1.0, 0.0).astype(BF)
    getz_ref[rows:] = jnp.where(hit_two & low, 1.0, 0.0).astype(BF)


def fan(send_ref, value, at):
    n_expert, n_fsdp = send_ref.shape[:2]
    width = value.shape[1]
    send_ref[:, :, :, at : at + width] = jnp.broadcast_to(
        value.reshape(n_expert, 1, 8, width), (n_expert, n_fsdp, 8, width)
    )


def place_body(put_ref, g_ref, send_ref):
    fan(send_ref, place(put_ref[...], g_ref[...]), 0)


def fan_body(spread_ref, send_ref):
    fan(send_ref, spread_ref[...], 0)


def place_both_body(spread_ref, put_ref, g_ref, send_ref):
    fan(send_ref, spread_ref[...], 0)
    fan(send_ref, place(put_ref[...], g_ref[...]), spread_ref.shape[1])


def join(mine, other, mask):
    value = jnp.where(mask, other, mine)
    rows, cols = value.shape
    turned = pltpu.roll(value.reshape(rows // 8, 8, cols), 4, 1).reshape(rows, cols)
    return value + turned


def forward(x, c, wg_ref, wu_ref):
    half, hid = wg_ref.shape[0] // 2, wg_ref.shape[1]
    c = jnp.concatenate([c.astype(F32)] * (hid // LANES), axis=1)
    mask = upper(x.shape[0], hid)
    a = join(dot(x, wg_ref[:half, :], NN), dot(x, wg_ref[half:, :], NN), mask)
    b = join(dot(x, wu_ref[:half, :], NN), dot(x, wu_ref[half:, :], NN), mask)
    sig = jax.nn.sigmoid(a)
    s = a * sig
    h = s * b
    return c * (b * (sig * (1.0 + a * (1.0 - sig)))), c * s, h, (c * h).astype(BF)


def backward(g, slope, act, hidden, wd_ref, wg_ref, wu_ref):
    half, hid = wg_ref.shape[0] // 2, wg_ref.shape[1]
    rows = g.shape[0]
    q = join(dot(g, wd_ref[:, :half], NT), dot(g, wd_ref[:, half:], NT), upper(rows, hid))
    da = (q * slope).astype(BF)
    db = (q * act).astype(BF)
    low = dot(da, wg_ref[:half, :], NT) + dot(db, wu_ref[:half, :], NT)
    high = dot(da, wg_ref[half:, :], NT) + dot(db, wu_ref[half:, :], NT)
    out = jnp.where(upper(rows, half), high, low).astype(BF)
    z = jnp.sum(q * hidden, axis=1, keepdims=True)
    return da, db, out, jnp.broadcast_to(z, (rows, LANES)).astype(BF)


def forward_body(rows_ref, wg_ref, wu_ref, slope_ref, act_ref, hid_ref, hg_ref, x_ref):
    half = wg_ref.shape[0] // 2
    x = rows_ref[:, :half]
    x_ref[...] = x
    slope, act, hidden, hg_ref[...] = forward(x, rows_ref[:, half:], wg_ref, wu_ref)
    slope_ref[...] = slope.astype(BF)
    act_ref[...] = act.astype(BF)
    hid_ref[...] = hidden.astype(BF)


def back_body(rows_ref, slope_ref, act_ref, hid_ref, wd_ref, wg_ref, wu_ref, out_ref, da_ref, db_ref, *z_ref):
    half = wg_ref.shape[0] // 2
    da_ref[...], db_ref[...], out, z = backward(
        rows_ref[...],
        slope_ref[...].astype(F32),
        act_ref[...].astype(F32),
        hid_ref[...].astype(F32),
        wd_ref,
        wg_ref,
        wu_ref,
    )
    out_ref[:, :half] = out
    if z_ref:
        z_ref[0][...] = z
    else:
        out_ref[:, half:] = z


def both_body(rows_ref, wd_ref, wg_ref, wu_ref, out_ref, da_ref, db_ref, z_ref, hg_ref, x_ref, g_ref):
    half = wg_ref.shape[0] // 2
    x = rows_ref[:, :half]
    g = rows_ref[:, half + LANES :]
    x_ref[...] = x
    g_ref[...] = g
    slope, act, hidden, hg_ref[...] = forward(x, rows_ref[:, half : half + LANES], wg_ref, wu_ref)
    da_ref[...], db_ref[...], out_ref[...], z_ref[...] = backward(g, slope, act, hidden, wd_ref, wg_ref, wu_ref)


def merge_body(get_ref, back_ref, g_ref, new_ref):
    tokens, width = g_ref.shape
    half = width // 2
    summed = dot(get_ref[...], back_ref[:, :half], NN)
    g = g_ref[...].astype(F32)
    new_ref[:, :half] = (g[:, :half] + summed[:tokens]).astype(BF)
    new_ref[:, half:] = (g[:, half:] + summed[tokens:]).astype(BF)


def gate_body(getz_ref, z_ref, gate_ref):
    _, micro, tok, top = gate_ref.shape
    value = dot(getz_ref[...], z_ref[:, z_ref.shape[1] - LANES :], NN)
    for m in range(micro):
        parts = [value[(k * micro + m) * tok : (k * micro + m + 1) * tok, 0:1] for k in range(top)]
        gate_ref[0, m] = jnp.concatenate(parts, axis=1)


def merge_gate_body(get_ref, getz_ref, back_ref, g_ref, new_ref, gate_ref):
    merge_body(get_ref, back_ref, g_ref, new_ref)
    gate_body(getz_ref, back_ref, gate_ref)


def outer_body(x_ref, g_ref, da_ref, db_ref, hg_ref, gate_ref, up_ref, down_ref):
    total, half = x_ref.shape
    hid = da_ref.shape[1]
    mask = upper(total, hid)
    x = x_ref[...]
    for k in range(2):
        at = slice(k * half, (k + 1) * half)
        keep = mask if k else ~mask
        only = lambda ref: jnp.where(keep, ref[...].astype(F32), 0.0).astype(BF)
        gate_ref[0, 0, at, :] = dot(x, only(da_ref), TN).astype(BF)
        up_ref[0, 0, at, :] = dot(x, only(db_ref), TN).astype(BF)
        down_ref[0, 0, :, at] = dot(only(hg_ref), g_ref[...], TN).astype(BF)


def local(acts, out_grad, expert_ids, gates, w_gate, w_up, w_down):
    segments = lax.axis_size("segment")
    segment = lax.axis_index("segment")
    n_expert = lax.axis_size("expert")
    n_fsdp = lax.axis_size("fsdp")
    _, micro, tok, width = acts.shape
    top = expert_ids.shape[3]
    cap = top * tok // n_expert
    tokens = micro * tok
    half = width // 2
    wide = half + LANES
    wg, wu, wd = w_gate[0, 0], w_up[0, 0], w_down[0, 0]
    hid = wg.shape[1]
    total = 8 * n_expert * n_fsdp
    sources = n_expert * n_fsdp
    last = segments - 1

    def exchange(value):
        cols = value.shape[-1]
        moved = lax.all_to_all(value.reshape(sources, 8, cols), ROUTE, 0, 0, tiled=True)
        return moved.reshape(total, cols)

    def rows_of(*cols):
        return [((total, c), BF) for c in cols]

    spread, put, get, getz = call(
        lambda *r: prep_body(micro, tok, cap, n_expert, n_fsdp, *r),
        [((8 * n_expert, wide), BF), ((tokens, 8 * n_expert), BF), ((2 * tokens, total), BF), ((top * tokens, total), BF)],
        expert_ids,
        gates,
        acts.reshape(tokens, width),
    )
    loss_grad = out_grad.reshape(tokens, width)

    def merge(back, grad):
        return call(merge_body, [((tokens, width), BF)], get, back, grad)[0]

    def gate_of(value):
        return call(gate_body, [((1, micro, tok, top), F32)], getz, value)[0]

    def outer(x_rows, g_rows, da, db, hg):
        cost = pl.CostEstimate(flops=12 * total * width * hid, bytes_accessed=12 * total * half, transcendentals=0)
        shapes = [(w_gate.shape, BF), (w_up.shape, BF), (w_down.shape, BF)]
        return tuple(call(outer_body, shapes, x_rows, g_rows, da, db, hg, cost=cost))

    def first():
        (send,) = call(
            place_both_body, [((n_expert, n_fsdp, 8, wide + half), BF)], spread, put, loss_grad
        )
        rows = exchange(send)
        out, da, db, z, hg, x_rows, g_rows = call_rows(
            both_body, rows_of(half, hid, hid, LANES, hid, half, half), [rows], [wd, wg, wu]
        )
        new = merge(exchange(out), loss_grad)
        unused = jnp.zeros((total, hid), BF)
        return (new, z, g_rows, da, db), (x_rows, unused, unused, unused, hg)

    def spread_out(value):
        return exchange(call(fan_body, [((n_expert, n_fsdp, 8, wide), BF)], value)[0])

    def gather_rows():
        lent = lax.ppermute(spread, "segment", [(last - 1, 0)])
        helped = lax.cond(segment == 0, spread_out, lambda v: jnp.zeros((total, wide), BF), lent)
        token = 1.0 + 0.0 * helped[0, :8].astype(F32)
        go = lax.ppermute(token, "segment", [(0, 1)])
        handed = lax.ppermute(helped, "segment", [(0, last - 1)])
        rows = lax.cond(
            (segment == 0) | (go[0] > 0.5), lambda v, e: spread_out(v), lambda v, e: e, spread, handed
        )
        slope, act, hidden, hg, x_rows = call_rows(
            forward_body, rows_of(hid, hid, hid, hid, half), [rows], [wg, wu]
        )
        state = (
            jnp.zeros((tokens, width), BF),
            jnp.zeros((total, LANES), BF),
            jnp.zeros((total, half), BF),
            jnp.zeros((total, hid), BF),
            jnp.zeros((total, hid), BF),
        )
        return state, (x_rows, slope, act, hidden, hg)

    state, saved = lax.cond(segment == last, first, gather_rows)
    x_rows, slope, act, hidden, hg = saved

    def dispatch(grad):
        (send,) = call(place_body, [((n_expert, n_fsdp, 8, half), BF)], put, grad)
        return exchange(send)

    def middle(grad, state):
        g_rows = dispatch(grad)
        out, da, db, z = call_rows(
            back_body, rows_of(half, hid, hid, LANES), [g_rows, slope, act, hidden], [wd, wg, wu]
        )
        new = merge(exchange(out), grad)
        return new, z, g_rows, da, db

    def final(grad, state):
        g_rows = dispatch(grad)
        out, da, db = call_rows(
            back_body, rows_of(wide, hid, hid), [g_rows, slope, act, hidden], [wd, wg, wu]
        )
        back = exchange(out)
        grads = outer(x_rows, g_rows, da, db, hg)
        new, gate = call(
            merge_gate_body,
            [((tokens, width), BF), ((1, micro, tok, top), F32)],
            get, getz, back, grad,
        )
        return (new, gate) + grads

    def finish(grad, state):
        new, z, g_rows, da, db = state
        return (new, gate_of(exchange(z))) + outer(x_rows, g_rows, da, db, hg)

    def step_down(layer, new):
        return lax.ppermute(new, "segment", [(layer, layer - 1)])

    grad = step_down(last, state[0])
    for layer in range(last - 1, 0, -1):
        state = lax.cond(segment == layer, middle, lambda g, s: s, grad, state)
        grad = step_down(layer, state[0])
    new, gate, grad_gate, grad_up, grad_down = lax.cond(segment == 0, final, finish, grad, state)
    return new.reshape(acts.shape), gate, grad_gate, grad_up, grad_down


def solution(mesh):
    in_specs = (
        P("segment", None, ("expert", "fsdp"), None),
        P(None, ("expert", "fsdp"), None),
        P("segment", None, ("expert", "fsdp"), None),
        P("segment", None, ("expert", "fsdp"), None),
        P("segment", "expert", None, "fsdp"),
        P("segment", "expert", None, "fsdp"),
        P("segment", "expert", "fsdp", None),
    )
    out_specs = (
        P("segment", None, ("expert", "fsdp"), None),
        P("segment", None, ("expert", "fsdp"), None),
        P("segment", "expert", None, "fsdp"),
        P("segment", "expert", None, "fsdp"),
        P("segment", "expert", "fsdp", None),
    )
    return jax.shard_map(local, mesh=mesh, in_specs=in_specs, out_specs=out_specs, check_vma=False)
```

```python
import jax
import jax.numpy as jnp
from jax import lax
from jax.experimental import pallas as pl
from jax.experimental.pallas import tpu as pltpu
from jax.sharding import PartitionSpec as P

BF = jnp.bfloat16
F32 = jnp.float32
NN = (((1,), (0,)), ((), ()))
NT = (((1,), (1,)), ((), ()))
TN = (((0,), (0,)), ((), ()))
LANES = 128
CHUNK = 512
SMALL = 128
ROUTE = ("expert", "fsdp")


def dot(a, b, dims):
    return lax.dot_general(a, b, dims, preferred_element_type=F32)


def iota(shape, dim):
    return lax.broadcasted_iota(jnp.int32, shape, dim)


def call(body, outs, *args, cost=None):
    return pl.pallas_call(
        body,
        out_shape=[jax.ShapeDtypeStruct(s, d) for s, d in outs],
        in_specs=[pl.BlockSpec(memory_space=pltpu.VMEM)] * len(args),
        out_specs=[pl.BlockSpec(memory_space=pltpu.VMEM)] * len(outs),
        compiler_params=pltpu.CompilerParams(vmem_limit_bytes=48 * 1024 * 1024),
        cost_estimate=cost,
    )(*args)


def call_rows(body, outs, streamed, whole, chunk=CHUNK):
    total = streamed[0].shape[0]
    by_rows = lambda shape: pl.BlockSpec((chunk, shape[1]), lambda i: (i, 0))
    return pl.pallas_call(
        body,
        grid=(total // chunk,),
        out_shape=[jax.ShapeDtypeStruct(s, d) for s, d in outs],
        in_specs=[by_rows(v.shape) for v in streamed] + [pl.BlockSpec(memory_space=pltpu.VMEM)] * len(whole),
        out_specs=[by_rows(s) for s, _ in outs],
        compiler_params=pltpu.CompilerParams(vmem_limit_bytes=48 * 1024 * 1024),
    )(*streamed, *whole)


def upper(rows, cols):
    return (iota((rows, cols), 0) % 8) >= 4


def place(routing, tokens):
    half = tokens.shape[1] // 2
    spread = dot(routing, tokens, TN)
    rows = spread.shape[0]
    return jnp.where(upper(rows, half), spread[:, half:], spread[:, :half]).astype(BF)


def prep_body(micro, tok, cap, n_expert, n_fsdp, ids_ref, gates_ref, x_ref, spread_ref, put_ref, get_ref, getz_ref, near_ref, nearz_ref):
    rows = micro * tok
    ids = jnp.concatenate([ids_ref[0, m] for m in range(micro)], axis=0)
    gates = jnp.concatenate([gates_ref[0, m].astype(F32) for m in range(micro)], axis=0)
    first, second = ids[:, 0:1], ids[:, 1:2]
    experts = iota((rows, LANES), 1)
    one, two = experts == first, experts == second
    counts = (one | two).astype(BF)
    r0, r1 = iota((rows, rows), 0), iota((rows, rows), 1)
    lower = ((r1 < r0) & (r1 // tok == r0 // tok)).astype(BF)
    before = dot(lower, counts, NN)
    place_of = iota((rows, 1), 0) // tok * cap
    slot_one = jnp.sum(jnp.where(one, before, 0.0), axis=1, keepdims=True).astype(jnp.int32) + place_of
    slot_two = jnp.sum(jnp.where(two, before, 0.0), axis=1, keepdims=True).astype(jnp.int32) + place_of
    cols = 8 * n_expert
    col = iota((rows, cols), 1)
    put_one = ((col // 8 == first) & (col % 4 == slot_one)).astype(F32)
    put_two = ((col // 8 == second) & (col % 4 == slot_two)).astype(F32)
    put = (put_one + put_two).astype(BF)
    put_ref[...] = put
    under = (col % 8) < 4
    near_ref[:rows] = jnp.where(under, put_one + put_two, 0.0).astype(BF)
    near_ref[rows:] = jnp.where(under, 0.0, put_one + put_two).astype(BF)
    nearz_ref[:rows] = jnp.where(under, put_one, 0.0).astype(BF)
    nearz_ref[rows:] = jnp.where(under, put_two, 0.0).astype(BF)
    put_gates = (put_one * gates[:, 0:1] + put_two * gates[:, 1:2]).astype(BF)
    half = x_ref.shape[1] // 2
    spread_ref[:, :half] = place(put, x_ref[...])
    spread_ref[:, half:] = dot(put_gates, jnp.ones((rows, LANES), BF), TN).astype(BF)
    total = 8 * n_expert * n_fsdp
    wide = iota((rows, total), 1)
    target = wide // (8 * n_fsdp)
    row = wide % 4
    low = (wide % 8) < 4
    hit_one = (target == first) & (row == slot_one)
    hit_two = (target == second) & (row == slot_two)
    hit = hit_one | hit_two
    get_ref[:rows] = jnp.where(hit & low, 1.0, 0.0).astype(BF)
    get_ref[rows:] = jnp.where(hit & ~low, 1.0, 0.0).astype(BF)
    getz_ref[:rows] = jnp.where(hit_one & low, 1.0, 0.0).astype(BF)
    getz_ref[rows:] = jnp.where(hit_two & low, 1.0, 0.0).astype(BF)


def fan(send_ref, value, at):
    n_expert, n_fsdp = send_ref.shape[:2]
    width = value.shape[1]
    send_ref[:, :, :, at : at + width] = jnp.broadcast_to(
        value.reshape(n_expert, 1, 8, width), (n_expert, n_fsdp, 8, width)
    )


def place_body(put_ref, g_ref, send_ref):
    fan(send_ref, place(put_ref[...], g_ref[...]), 0)


def fan_body(spread_ref, send_ref):
    fan(send_ref, spread_ref[...], 0)


def place_both_body(spread_ref, put_ref, g_ref, send_ref):
    fan(send_ref, spread_ref[...], 0)
    fan(send_ref, place(put_ref[...], g_ref[...]), spread_ref.shape[1])


def join(mine, other, mask):
    value = jnp.where(mask, other, mine)
    rows, cols = value.shape
    turned = pltpu.roll(value.reshape(rows // 8, 8, cols), 4, 1).reshape(rows, cols)
    return value + turned


def forward(x, c, wg_ref, wu_ref):
    half, hid = wg_ref.shape[0] // 2, wg_ref.shape[1]
    c = jnp.concatenate([c.astype(F32)] * (hid // LANES), axis=1)
    mask = upper(x.shape[0], hid)
    a = join(dot(x, wg_ref[:half, :], NN), dot(x, wg_ref[half:, :], NN), mask)
    b = join(dot(x, wu_ref[:half, :], NN), dot(x, wu_ref[half:, :], NN), mask)
    sig = jax.nn.sigmoid(a)
    s = a * sig
    h = s * b
    return c * (b * (sig * (1.0 + a * (1.0 - sig)))), c * s, h, (c * h).astype(BF)


def backward(g, slope, act, hidden, wd_ref, wg_ref, wu_ref):
    half, hid = wg_ref.shape[0] // 2, wg_ref.shape[1]
    rows = g.shape[0]
    q = join(dot(g, wd_ref[:, :half], NT), dot(g, wd_ref[:, half:], NT), upper(rows, hid))
    da = (q * slope).astype(BF)
    db = (q * act).astype(BF)
    low = dot(da, wg_ref[:half, :], NT) + dot(db, wu_ref[:half, :], NT)
    high = dot(da, wg_ref[half:, :], NT) + dot(db, wu_ref[half:, :], NT)
    out = jnp.where(upper(rows, half), high, low).astype(BF)
    z = jnp.sum(q * hidden, axis=1, keepdims=True)
    return da, db, out, jnp.broadcast_to(z, (rows, LANES)).astype(BF)


def forward_body(rows_ref, wg_ref, wu_ref, slope_ref, act_ref, hid_ref, hg_ref, x_ref):
    half = wg_ref.shape[0] // 2
    x = rows_ref[:, :half]
    x_ref[...] = x
    slope, act, hidden, hg_ref[...] = forward(x, rows_ref[:, half:], wg_ref, wu_ref)
    slope_ref[...] = slope.astype(BF)
    act_ref[...] = act.astype(BF)
    hid_ref[...] = hidden.astype(BF)


def back_body(rows_ref, slope_ref, act_ref, hid_ref, wd_ref, wg_ref, wu_ref, out_ref, da_ref, db_ref, *z_ref):
    half = wg_ref.shape[0] // 2
    da_ref[...], db_ref[...], out, z = backward(
        rows_ref[...],
        slope_ref[...].astype(F32),
        act_ref[...].astype(F32),
        hid_ref[...].astype(F32),
        wd_ref,
        wg_ref,
        wu_ref,
    )
    out_ref[:, :half] = out
    if z_ref:
        z_ref[0][...] = z
    else:
        out_ref[:, half:] = z


def grad_body(rows_ref, slope_ref, act_ref, wd_ref, da_ref, db_ref):
    half = wd_ref.shape[1] // 2
    g = rows_ref[...]
    mask = upper(g.shape[0], wd_ref.shape[0])
    q = join(dot(g, wd_ref[:, :half], NT), dot(g, wd_ref[:, half:], NT), mask)
    da_ref[...] = (q * slope_ref[...].astype(F32)).astype(BF)
    db_ref[...] = (q * act_ref[...].astype(F32)).astype(BF)


def both_body(rows_ref, wd_ref, wg_ref, wu_ref, out_ref, da_ref, db_ref, z_ref, hg_ref, x_ref, g_ref):
    half = wg_ref.shape[0] // 2
    x = rows_ref[:, :half]
    g = rows_ref[:, half + LANES :]
    x_ref[...] = x
    g_ref[...] = g
    slope, act, hidden, hg_ref[...] = forward(x, rows_ref[:, half : half + LANES], wg_ref, wu_ref)
    da_ref[...], db_ref[...], out_ref[...], z_ref[...] = backward(g, slope, act, hidden, wd_ref, wg_ref, wu_ref)


def nothing_body(*refs):
    pass


def near_place_body(put_ref, g_ref, send_ref):
    send_ref[...] = place(put_ref[...], g_ref[...])


def near_forward_body(rows_ref, w_ref, slope_ref, act_ref, hid_ref):
    half = w_ref.shape[2] // 2
    slope, act, hidden, _ = forward(rows_ref[:, :half], rows_ref[:, half:], w_ref.at[0, 0], w_ref.at[0, 1])
    slope_ref[0] = slope.astype(BF)
    act_ref[0] = act.astype(BF)
    hid_ref[0] = hidden.astype(BF)


def near_back_body(g_ref, slope_ref, act_ref, hid_ref, w_ref, out_ref, low_ref, high_ref, z_ref):
    half, hid = w_ref.shape[2] // 2, w_ref.shape[3]
    rows = g_ref.shape[0]
    block = pl.program_id(0)

    @pl.when(block == 0)
    def _():
        low_ref[...] = jnp.zeros_like(low_ref)
        high_ref[...] = jnp.zeros_like(high_ref)
        z_ref[...] = jnp.zeros_like(z_ref)

    g = g_ref[...]
    q = join(dot(g, w_ref[0, 2, :half, :], NN), dot(g, w_ref[0, 2, half:, :], NN), upper(rows, hid))
    da = (q * slope_ref[0].astype(F32)).astype(BF)
    db = (q * act_ref[0].astype(F32)).astype(BF)
    low_ref[...] += dot(da, w_ref[0, 0, :half, :], NT) + dot(db, w_ref[0, 1, :half, :], NT)
    high_ref[...] += dot(da, w_ref[0, 0, half:, :], NT) + dot(db, w_ref[0, 1, half:, :], NT)
    z = jnp.sum(q * hid_ref[0].astype(F32), axis=1, keepdims=True)
    z_ref[...] += jnp.broadcast_to(z, z_ref.shape)

    @pl.when(block == pl.num_programs(0) - 1)
    def _():
        out_ref[:, :half] = jnp.where(upper(rows, half), high_ref[...], low_ref[...]).astype(BF)
        out_ref[:, half:] = z_ref[...].astype(BF)


def merge_body(get_ref, back_ref, g_ref, new_ref):
    tokens, width = g_ref.shape
    half = width // 2
    summed = dot(get_ref[...], back_ref[:, :half], NN)
    g = g_ref[...].astype(F32)
    new_ref[:, :half] = (g[:, :half] + summed[:tokens]).astype(BF)
    new_ref[:, half:] = (g[:, half:] + summed[tokens:]).astype(BF)


def gate_body(getz_ref, z_ref, gate_ref):
    _, micro, tok, top = gate_ref.shape
    value = dot(getz_ref[...], z_ref[:, z_ref.shape[1] - LANES :], NN)
    for m in range(micro):
        parts = [value[(k * micro + m) * tok : (k * micro + m + 1) * tok, 0:1] for k in range(top)]
        gate_ref[0, m] = jnp.concatenate(parts, axis=1)


def merge_gate_body(get_ref, getz_ref, back_ref, g_ref, new_ref, gate_ref):
    merge_body(get_ref, back_ref, g_ref, new_ref)
    gate_body(getz_ref, back_ref, gate_ref)


def outer_body(x_ref, g_ref, da_ref, db_ref, hg_ref, gate_ref, up_ref, down_ref):
    total, half = x_ref.shape
    hid = da_ref.shape[1]
    mask = upper(total, hid)
    x = x_ref[...]
    for k in range(2):
        at = slice(k * half, (k + 1) * half)
        keep = mask if k else ~mask
        only = lambda ref: jnp.where(keep, ref[...].astype(F32), 0.0).astype(BF)
        gate_ref[0, 0, at, :] = dot(x, only(da_ref), TN).astype(BF)
        up_ref[0, 0, at, :] = dot(x, only(db_ref), TN).astype(BF)
        down_ref[0, 0, :, at] = dot(only(hg_ref), g_ref[...], TN).astype(BF)


def local(acts, out_grad, expert_ids, gates, w_gate, w_up, w_down):
    segments = lax.axis_size("segment")
    segment = lax.axis_index("segment")
    n_expert = lax.axis_size("expert")
    n_fsdp = lax.axis_size("fsdp")
    _, micro, tok, width = acts.shape
    top = expert_ids.shape[3]
    cap = top * tok // n_expert
    tokens = micro * tok
    half = width // 2
    wide = half + LANES
    wg, wu, wd = w_gate[0, 0], w_up[0, 0], w_down[0, 0]
    hid = wg.shape[1]
    total = 8 * n_expert * n_fsdp
    sources = n_expert * n_fsdp
    last = segments - 1

    def exchange(value):
        cols = value.shape[-1]
        moved = lax.all_to_all(value.reshape(sources, 8, cols), ROUTE, 0, 0, tiled=True)
        return moved.reshape(total, cols)

    def unfilled(*shapes):
        return pl.pallas_call(
            nothing_body,
            out_shape=[jax.ShapeDtypeStruct(s, d) for s, d in shapes],
            out_specs=[pl.BlockSpec(memory_space=pl.ANY)] * len(shapes),
        )()

    def by_block(body, outs, args, whole, scratch=()):
        one = lambda v: pl.BlockSpec((1,) + v[1:], lambda i: (i,) + (0,) * (len(v) - 1))
        stay = lambda v: pl.BlockSpec(v, lambda i: (0,) * len(v))
        return pl.pallas_call(
            body,
            grid=(n_fsdp,),
            out_shape=[jax.ShapeDtypeStruct(v, d) for v, d in outs],
            in_specs=[stay(v.shape) for v in whole] + [one(v.shape) for v in args],
            out_specs=[one(v) if len(v) > 2 else stay(v) for v, _ in outs],
            scratch_shapes=[pltpu.VMEM(v, F32) for v in scratch],
            compiler_params=pltpu.CompilerParams(vmem_limit_bytes=48 * 1024 * 1024),
        )(*whole, *args)

    def shift(value, steps):
        pairs = [(k, (k + steps) % n_fsdp) for k in range(n_fsdp)]
        return lax.ppermute(value, "fsdp", pairs)

    def ring(own):
        ahead, behind = [own], [own]
        for step in range(n_fsdp // 2):
            ahead.append(shift(ahead[-1], 1))
            if step < n_fsdp // 2 - 1:
                behind.append(shift(behind[-1], -1))
        return ahead + behind[:0:-1]

    def near(value):
        return value.reshape(n_expert, n_fsdp, 8, value.shape[-1])

    def rows_of(*cols):
        return [((total, c), BF) for c in cols]

    spread, put, get, getz, near_get, near_getz = call(
        lambda *r: prep_body(micro, tok, cap, n_expert, n_fsdp, *r),
        [((8 * n_expert, wide), BF), ((tokens, 8 * n_expert), BF), ((2 * tokens, total), BF), ((top * tokens, total), BF)]
        + [((2 * tokens, 8 * n_expert), BF), ((top * tokens, 8 * n_expert), BF)],
        expert_ids,
        gates,
        acts.reshape(tokens, width),
    )
    loss_grad = out_grad.reshape(tokens, width)

    def merge(back, grad):
        return call(merge_body, [((tokens, width), BF)], get, back, grad)[0]

    def gate_of(value):
        return call(gate_body, [((1, micro, tok, top), F32)], getz, value)[0]

    def outer(x_rows, g_rows, da, db, hg):
        cost = pl.CostEstimate(flops=12 * total * width * hid, bytes_accessed=12 * total * half, transcendentals=0)
        shapes = [(w_gate.shape, BF), (w_up.shape, BF), (w_down.shape, BF)]
        return tuple(call(outer_body, shapes, x_rows, g_rows, da, db, hg, cost=cost))

    fsdp_now = lax.axis_index("fsdp")
    near_rows = 8 * n_expert
    blocks = (3, width, hid)
    def first():
        (send,) = call(
            place_both_body, [((n_expert, n_fsdp, 8, wide + half), BF)], spread, put, loss_grad
        )
        rows = exchange(send)
        out, da, db, z, hg, x_rows, g_rows = call_rows(
            both_body, rows_of(half, hid, hid, LANES, hid, half, half), [rows], [wd, wg, wu]
        )
        new = merge(exchange(out), loss_grad)
        unused = unfilled(
            ((total, hid), BF), ((total, hid), BF), ((total, hid), BF), ((near_rows, wide), BF), *[(blocks, BF)] * n_fsdp
        )
        return (new, z, g_rows, da, db), (x_rows, *unused[:3], hg), unused[3], tuple(unused[4:])

    def spread_out(value):
        return exchange(call(fan_body, [((n_expert, n_fsdp, 8, wide), BF)], value)[0])

    def gather_rows():
        lent = lax.ppermute(spread, "segment", [(last - 1, 0)])
        helped = lax.cond(segment == 0, spread_out, lambda v: jnp.zeros((total, wide), BF), lent)
        token = 1.0 + 0.0 * helped[0, :8].astype(F32)
        go = lax.ppermute(token, "segment", [(0, 1)])
        handed = lax.ppermute(helped, "segment", [(0, last - 1)])
        pieces = lax.cond(
            segment == 1,
            lambda: tuple(ring(jnp.stack([wg, wu, wd.T]))),
            lambda: tuple(unfilled(*[(blocks, BF)] * n_fsdp)),
        )
        far = pieces[n_fsdp // 2][0, 0, 0].astype(F32)
        rows = lax.cond(
            (segment == 0) | ((go[0] > 0.5) & (jnp.abs(far) < 1e30)), lambda v, e: spread_out(v), lambda v, e: e, spread, handed
        )
        slope, act, hidden, hg, x_rows = call_rows(
            forward_body, rows_of(hid, hid, hid, hid, half), [rows], [wg, wu], SMALL
        )
        plane = lax.dynamic_index_in_dim(near(rows), fsdp_now, 1, keepdims=False).reshape(near_rows, wide)
        state = unfilled(
            ((tokens, width), BF), ((total, LANES), BF), ((total, half), BF), ((total, hid), BF), ((total, hid), BF)
        )
        return tuple(state), (x_rows, slope, act, hidden, hg), plane, pieces

    state, saved, plane, pieces = lax.cond(segment == last, first, gather_rows)
    x_rows, slope, act, hidden, hg = saved

    def dispatch(grad):
        (send,) = call(place_body, [((n_expert, n_fsdp, 8, half), BF)], put, grad)
        return exchange(send)

    near_shape = ((n_fsdp, near_rows, hid), BF)

    def near_forward(plane, pieces):
        whole = jnp.stack(pieces)
        return (whole, *by_block(near_forward_body, [near_shape] * 3, [whole], [plane]))

    whole, near_slope, near_act, near_hid = lax.cond(
        segment == 1,
        near_forward,
        lambda *_: tuple(unfilled(((n_fsdp,) + blocks, BF), near_shape, near_shape, near_shape)),
        plane,
        pieces,
    )

    def exchange_near(value):
        cols = value.shape[-1]
        moved = lax.all_to_all(value.reshape(n_expert, 8, cols), "expert", 0, 0, tiled=True)
        return moved.reshape(near_rows, cols)

    gate_shape = ((1, micro, tok, top), F32)

    def relay(grad, new):
        (send,) = call(near_place_body, [((near_rows, half), BF)], put, grad)
        g_near = exchange_near(send)
        (out,) = by_block(
            near_back_body,
            [((near_rows, wide), BF)],
            [near_slope, near_act, near_hid, whole],
            [g_near],
            [(near_rows, half), (near_rows, half), (near_rows, LANES)],
        )
        back = exchange_near(out)
        new, gate = call(
            merge_gate_body, [((tokens, width), BF), gate_shape], near_get, near_getz, back, grad
        )
        return new, g_near, gate

    def relay_not(grad, new):
        return (new, *unfilled(((near_rows, half), BF), gate_shape))

    def middle(grad, state):
        g_rows = dispatch(grad)
        out, da, db, z = call_rows(
            back_body, rows_of(half, hid, hid, LANES), [g_rows, slope, act, hidden], [wd, wg, wu]
        )
        new = merge(exchange(out), grad)
        return new, z, g_rows, da, db

    def final(grad, state, done):
        g_rows = dispatch(grad)
        out, da, db = call_rows(
            back_body, rows_of(wide, hid, hid), [g_rows, slope, act, hidden], [wd, wg, wu]
        )
        back = exchange(out)
        grads = outer(x_rows, g_rows, da, db, hg)
        new, gate = call(
            merge_gate_body, [((tokens, width), BF), gate_shape], get, getz, back, grad
        )
        return (new, gate) + grads

    def collect(state, done):
        new, g_near, gate, _ = done
        g_all = jnp.zeros((n_expert, n_fsdp, 8, half), BF)
        for k, piece in enumerate(ring(g_near)):
            at = (0, (fsdp_now - k) % n_fsdp, 0, 0)
            g_all = lax.dynamic_update_slice(g_all, piece.reshape(n_expert, 1, 8, half), at)
        g_rows = g_all.reshape(total, half)
        da, db = call_rows(grad_body, rows_of(hid, hid), [g_rows, slope, act], [wd], SMALL)
        return gate, g_rows, da, db

    def settle(state, done):
        _, z, g_rows, da, db = state
        z = z + (0.0 * done[3][0]).astype(BF)
        return gate_of(exchange(z)), g_rows, da, db

    def finish(grad, state, done):
        gate, g_rows, da, db = lax.cond(segment == 1, collect, settle, state, done)
        return (done[0], gate) + outer(x_rows, g_rows, da, db, hg)

    def step_down(layer, new):
        return lax.ppermute(new, "segment", [(layer, layer - 1)])

    grad = step_down(last, state[0])
    for layer in range(last - 1, 1, -1):
        state = lax.cond(segment == layer, middle, lambda g, s: s, grad, state)
        grad = step_down(layer, state[0])
    new, g_near, gate = lax.cond(segment == 1, relay, relay_not, grad, state[0])
    grad = step_down(1, new)
    hold = lax.ppermute(1.0 + 0.0 * new[0, :8].astype(F32), "segment", [(1, last)])
    new, gate, grad_gate, grad_up, grad_down = lax.cond(
        segment == 0, final, finish, grad, state, (new, g_near, gate, hold)
    )
    return new.reshape(acts.shape), gate, grad_gate, grad_up, grad_down


def solution(mesh):
    in_specs = (
        P("segment", None, ("expert", "fsdp"), None),
        P(None, ("expert", "fsdp"), None),
        P("segment", None, ("expert", "fsdp"), None),
        P("segment", None, ("expert", "fsdp"), None),
        P("segment", "expert", None, "fsdp"),
        P("segment", "expert", None, "fsdp"),
        P("segment", "expert", "fsdp", None),
    )
    out_specs = (
        P("segment", None, ("expert", "fsdp"), None),
        P("segment", None, ("expert", "fsdp"), None),
        P("segment", "expert", None, "fsdp"),
        P("segment", "expert", None, "fsdp"),
        P("segment", "expert", "fsdp", None),
    )
    return jax.shard_map(local, mesh=mesh, in_specs=in_specs, out_specs=out_specs, check_vma=False)
```

```python
import jax
import jax.numpy as jnp
from jax import lax
from jax.experimental import pallas as pl
from jax.experimental.pallas import tpu as pltpu
from jax.sharding import PartitionSpec as P

BF = jnp.bfloat16
F32 = jnp.float32
NN = (((1,), (0,)), ((), ()))
NT = (((1,), (1,)), ((), ()))
TN = (((0,), (0,)), ((), ()))
LANES = 128
CHUNK = 512
SMALL = 128
ROUTE = ("expert", "fsdp")


def dot(a, b, dims):
    return lax.dot_general(a, b, dims, preferred_element_type=F32)


def iota(shape, dim):
    return lax.broadcasted_iota(jnp.int32, shape, dim)


def call(body, outs, *args, cost=None):
    return pl.pallas_call(
        body,
        out_shape=[jax.ShapeDtypeStruct(s, d) for s, d in outs],
        in_specs=[pl.BlockSpec(memory_space=pltpu.VMEM)] * len(args),
        out_specs=[pl.BlockSpec(memory_space=pltpu.VMEM)] * len(outs),
        compiler_params=pltpu.CompilerParams(vmem_limit_bytes=48 * 1024 * 1024),
        cost_estimate=cost,
    )(*args)


def call_rows(body, outs, streamed, whole, chunk=CHUNK):
    total = streamed[0].shape[0]
    by_rows = lambda shape: pl.BlockSpec((chunk, shape[1]), lambda i: (i, 0))
    return pl.pallas_call(
        body,
        grid=(total // chunk,),
        out_shape=[jax.ShapeDtypeStruct(s, d) for s, d in outs],
        in_specs=[by_rows(v.shape) for v in streamed] + [pl.BlockSpec(memory_space=pltpu.VMEM)] * len(whole),
        out_specs=[by_rows(s) for s, _ in outs],
        compiler_params=pltpu.CompilerParams(vmem_limit_bytes=48 * 1024 * 1024),
    )(*streamed, *whole)


def upper(rows, cols):
    return (iota((rows, cols), 0) % 8) >= 4


def place(routing, tokens):
    half = tokens.shape[1] // 2
    spread = dot(routing, tokens, TN)
    rows = spread.shape[0]
    return jnp.where(upper(rows, half), spread[:, half:], spread[:, :half]).astype(BF)


def prep_body(micro, tok, cap, n_expert, n_fsdp, ids_ref, gates_ref, x_ref, spread_ref, put_ref, get_ref, getz_ref, near_ref, nearz_ref):
    rows = micro * tok
    ids = jnp.concatenate([ids_ref[0, m] for m in range(micro)], axis=0)
    gates = jnp.concatenate([gates_ref[0, m].astype(F32) for m in range(micro)], axis=0)
    first, second = ids[:, 0:1], ids[:, 1:2]
    experts = iota((rows, LANES), 1)
    one, two = experts == first, experts == second
    counts = (one | two).astype(BF)
    r0, r1 = iota((rows, rows), 0), iota((rows, rows), 1)
    lower = ((r1 < r0) & (r1 // tok == r0 // tok)).astype(BF)
    before = dot(lower, counts, NN)
    place_of = iota((rows, 1), 0) // tok * cap
    slot_one = jnp.sum(jnp.where(one, before, 0.0), axis=1, keepdims=True).astype(jnp.int32) + place_of
    slot_two = jnp.sum(jnp.where(two, before, 0.0), axis=1, keepdims=True).astype(jnp.int32) + place_of
    cols = 8 * n_expert
    col = iota((rows, cols), 1)
    put_one = ((col // 8 == first) & (col % 4 == slot_one)).astype(F32)
    put_two = ((col // 8 == second) & (col % 4 == slot_two)).astype(F32)
    put = (put_one + put_two).astype(BF)
    put_ref[...] = put
    under = (col % 8) < 4
    near_ref[:rows] = jnp.where(under, put_one + put_two, 0.0).astype(BF)
    near_ref[rows:] = jnp.where(under, 0.0, put_one + put_two).astype(BF)
    nearz_ref[:rows] = jnp.where(under, put_one, 0.0).astype(BF)
    nearz_ref[rows:] = jnp.where(under, put_two, 0.0).astype(BF)
    put_gates = (put_one * gates[:, 0:1] + put_two * gates[:, 1:2]).astype(BF)
    half = x_ref.shape[1] // 2
    spread_ref[:, :half] = place(put, x_ref[...])
    spread_ref[:, half:] = dot(put_gates, jnp.ones((rows, LANES), BF), TN).astype(BF)
    total = 8 * n_expert * n_fsdp
    wide = iota((rows, total), 1)
    target = wide // (8 * n_fsdp)
    row = wide % 4
    low = (wide % 8) < 4
    hit_one = (target == first) & (row == slot_one)
    hit_two = (target == second) & (row == slot_two)
    hit = hit_one | hit_two
    get_ref[:rows] = jnp.where(hit & low, 1.0, 0.0).astype(BF)
    get_ref[rows:] = jnp.where(hit & ~low, 1.0, 0.0).astype(BF)
    getz_ref[:rows] = jnp.where(hit_one & low, 1.0, 0.0).astype(BF)
    getz_ref[rows:] = jnp.where(hit_two & low, 1.0, 0.0).astype(BF)


def fan(send_ref, value, at):
    n_expert, n_fsdp = send_ref.shape[:2]
    width = value.shape[1]
    send_ref[:, :, :, at : at + width] = jnp.broadcast_to(
        value.reshape(n_expert, 1, 8, width), (n_expert, n_fsdp, 8, width)
    )


def place_body(put_ref, g_ref, send_ref):
    fan(send_ref, place(put_ref[...], g_ref[...]), 0)


def fan_body(spread_ref, send_ref):
    fan(send_ref, spread_ref[...], 0)


def place_both_body(spread_ref, put_ref, g_ref, send_ref):
    fan(send_ref, spread_ref[...], 0)
    fan(send_ref, place(put_ref[...], g_ref[...]), spread_ref.shape[1])


def join(mine, other, mask):
    value = jnp.where(mask, other, mine)
    rows, cols = value.shape
    turned = pltpu.roll(value.reshape(rows // 8, 8, cols), 4, 1).reshape(rows, cols)
    return value + turned


def forward(x, c, wg_ref, wu_ref):
    half, hid = wg_ref.shape[0] // 2, wg_ref.shape[1]
    c = jnp.concatenate([c.astype(F32)] * (hid // LANES), axis=1)
    mask = upper(x.shape[0], hid)
    a = join(dot(x, wg_ref[:half, :], NN), dot(x, wg_ref[half:, :], NN), mask)
    b = join(dot(x, wu_ref[:half, :], NN), dot(x, wu_ref[half:, :], NN), mask)
    sig = jax.nn.sigmoid(a)
    s = a * sig
    h = s * b
    return c * (b * (sig * (1.0 + a * (1.0 - sig)))), c * s, h, (c * h).astype(BF)


def backward(g, slope, act, hidden, wd_ref, wg_ref, wu_ref):
    half, hid = wg_ref.shape[0] // 2, wg_ref.shape[1]
    rows = g.shape[0]
    q = join(dot(g, wd_ref[:, :half], NT), dot(g, wd_ref[:, half:], NT), upper(rows, hid))
    da = (q * slope).astype(BF)
    db = (q * act).astype(BF)
    low = dot(da, wg_ref[:half, :], NT) + dot(db, wu_ref[:half, :], NT)
    high = dot(da, wg_ref[half:, :], NT) + dot(db, wu_ref[half:, :], NT)
    out = jnp.where(upper(rows, half), high, low).astype(BF)
    z = jnp.sum(q * hidden, axis=1, keepdims=True)
    return da, db, out, jnp.broadcast_to(z, (rows, LANES)).astype(BF)


def forward_body(rows_ref, wg_ref, wu_ref, slope_ref, act_ref, hid_ref, hg_ref, x_ref):
    half = wg_ref.shape[0] // 2
    x = rows_ref[:, :half]
    x_ref[...] = x
    slope, act, hidden, hg_ref[...] = forward(x, rows_ref[:, half:], wg_ref, wu_ref)
    slope_ref[...] = slope.astype(BF)
    act_ref[...] = act.astype(BF)
    hid_ref[...] = hidden.astype(BF)


def back_body(rows_ref, slope_ref, act_ref, hid_ref, wd_ref, wg_ref, wu_ref, out_ref, da_ref, db_ref, *z_ref):
    half = wg_ref.shape[0] // 2
    da_ref[...], db_ref[...], out, z = backward(
        rows_ref[...],
        slope_ref[...].astype(F32),
        act_ref[...].astype(F32),
        hid_ref[...].astype(F32),
        wd_ref,
        wg_ref,
        wu_ref,
    )
    out_ref[:, :half] = out
    if z_ref:
        z_ref[0][...] = z
    else:
        out_ref[:, half:] = z


def grad_body(rows_ref, slope_ref, act_ref, wd_ref, da_ref, db_ref):
    half = wd_ref.shape[1] // 2
    g = rows_ref[...]
    mask = upper(g.shape[0], wd_ref.shape[0])
    q = join(dot(g, wd_ref[:, :half], NT), dot(g, wd_ref[:, half:], NT), mask)
    da_ref[...] = (q * slope_ref[...].astype(F32)).astype(BF)
    db_ref[...] = (q * act_ref[...].astype(F32)).astype(BF)


def both_body(rows_ref, wd_ref, wg_ref, wu_ref, out_ref, da_ref, db_ref, z_ref, hg_ref, x_ref, g_ref):
    half = wg_ref.shape[0] // 2
    x = rows_ref[:, :half]
    g = rows_ref[:, half + LANES :]
    x_ref[...] = x
    g_ref[...] = g
    slope, act, hidden, hg_ref[...] = forward(x, rows_ref[:, half : half + LANES], wg_ref, wu_ref)
    da_ref[...], db_ref[...], out_ref[...], z_ref[...] = backward(g, slope, act, hidden, wd_ref, wg_ref, wu_ref)


def nothing_body(*refs):
    pass


def near_place_body(put_ref, g_ref, send_ref):
    send_ref[...] = place(put_ref[...], g_ref[...])


def near_forward_body(rows_ref, w_ref, slope_ref, act_ref, hid_ref):
    half = w_ref.shape[3] // 2
    x, c = rows_ref[:, :half], rows_ref[:, half:]
    c = jnp.concatenate([c.astype(F32)] * (w_ref.shape[2] // LANES), axis=1)
    mask = upper(*c.shape)
    a = join(dot(x, w_ref[0, 0, :, :half], NT), dot(x, w_ref[0, 0, :, half:], NT), mask)
    b = join(dot(x, w_ref[0, 1, :, :half], NT), dot(x, w_ref[0, 1, :, half:], NT), mask)
    sig = jax.nn.sigmoid(a)
    s = a * sig
    slope_ref[0] = (c * (b * (sig * (1.0 + a * (1.0 - sig))))).astype(BF)
    act_ref[0] = (c * s).astype(BF)
    hid_ref[0] = (s * b).astype(BF)


def near_back_body(g_ref, slope_ref, act_ref, hid_ref, w_ref, out_ref, low_ref, high_ref, z_ref):
    half, hid = w_ref.shape[3] // 2, w_ref.shape[2]
    rows = g_ref.shape[0]
    block = pl.program_id(0)

    @pl.when(block == 0)
    def _():
        low_ref[...] = jnp.zeros_like(low_ref)
        high_ref[...] = jnp.zeros_like(high_ref)
        z_ref[...] = jnp.zeros_like(z_ref)

    g = g_ref[...]
    q = join(dot(g, w_ref[0, 2, :, :half], NT), dot(g, w_ref[0, 2, :, half:], NT), upper(rows, hid))
    da = (q * slope_ref[0].astype(F32)).astype(BF)
    db = (q * act_ref[0].astype(F32)).astype(BF)
    low_ref[...] += dot(da, w_ref[0, 0, :, :half], NN) + dot(db, w_ref[0, 1, :, :half], NN)
    high_ref[...] += dot(da, w_ref[0, 0, :, half:], NN) + dot(db, w_ref[0, 1, :, half:], NN)
    z = jnp.sum(q * hid_ref[0].astype(F32), axis=1, keepdims=True)
    z_ref[...] += jnp.broadcast_to(z, z_ref.shape)

    @pl.when(block == pl.num_programs(0) - 1)
    def _():
        out_ref[:, :half] = jnp.where(upper(rows, half), high_ref[...], low_ref[...]).astype(BF)
        out_ref[:, half:] = z_ref[...].astype(BF)


def merge_body(get_ref, back_ref, g_ref, new_ref):
    tokens, width = g_ref.shape
    half = width // 2
    summed = dot(get_ref[...], back_ref[:, :half], NN)
    g = g_ref[...].astype(F32)
    new_ref[:, :half] = (g[:, :half] + summed[:tokens]).astype(BF)
    new_ref[:, half:] = (g[:, half:] + summed[tokens:]).astype(BF)


def gate_body(getz_ref, z_ref, gate_ref):
    _, micro, tok, top = gate_ref.shape
    value = dot(getz_ref[...], z_ref[:, z_ref.shape[1] - LANES :], NN)
    for m in range(micro):
        parts = [value[(k * micro + m) * tok : (k * micro + m + 1) * tok, 0:1] for k in range(top)]
        gate_ref[0, m] = jnp.concatenate(parts, axis=1)


def merge_gate_body(get_ref, getz_ref, back_ref, g_ref, new_ref, gate_ref):
    merge_body(get_ref, back_ref, g_ref, new_ref)
    gate_body(getz_ref, back_ref, gate_ref)


def outer_body(x_ref, g_ref, da_ref, db_ref, hg_ref, gate_ref, up_ref, down_ref):
    total, half = x_ref.shape
    hid = da_ref.shape[1]
    mask = upper(total, hid)
    x = x_ref[...]
    for k in range(2):
        at = slice(k * half, (k + 1) * half)
        keep = mask if k else ~mask
        only = lambda ref: jnp.where(keep, ref[...].astype(F32), 0.0).astype(BF)
        gate_ref[0, 0, at, :] = dot(x, only(da_ref), TN).astype(BF)
        up_ref[0, 0, at, :] = dot(x, only(db_ref), TN).astype(BF)
        down_ref[0, 0, :, at] = dot(only(hg_ref), g_ref[...], TN).astype(BF)


def local(acts, out_grad, expert_ids, gates, w_gate, w_up, w_down):
    segments = lax.axis_size("segment")
    segment = lax.axis_index("segment")
    n_expert = lax.axis_size("expert")
    n_fsdp = lax.axis_size("fsdp")
    _, micro, tok, width = acts.shape
    top = expert_ids.shape[3]
    cap = top * tok // n_expert
    tokens = micro * tok
    half = width // 2
    wide = half + LANES
    wg, wu, wd = w_gate[0, 0], w_up[0, 0], w_down[0, 0]
    hid = wg.shape[1]
    total = 8 * n_expert * n_fsdp
    sources = n_expert * n_fsdp
    last = segments - 1

    def exchange(value):
        cols = value.shape[-1]
        moved = lax.all_to_all(value.reshape(sources, 8, cols), ROUTE, 0, 0, tiled=True)
        return moved.reshape(total, cols)

    def unfilled(*shapes):
        return pl.pallas_call(
            nothing_body,
            out_shape=[jax.ShapeDtypeStruct(s, d) for s, d in shapes],
            out_specs=[pl.BlockSpec(memory_space=pl.ANY)] * len(shapes),
        )()

    def by_block(body, outs, args, whole, scratch=()):
        one = lambda v: pl.BlockSpec((1,) + v[1:], lambda i: (i,) + (0,) * (len(v) - 1))
        stay = lambda v: pl.BlockSpec(v, lambda i: (0,) * len(v))
        return pl.pallas_call(
            body,
            grid=(n_fsdp,),
            out_shape=[jax.ShapeDtypeStruct(v, d) for v, d in outs],
            in_specs=[stay(v.shape) for v in whole] + [one(v.shape) for v in args],
            out_specs=[one(v) if len(v) > 2 else stay(v) for v, _ in outs],
            scratch_shapes=[pltpu.VMEM(v, F32) for v in scratch],
            compiler_params=pltpu.CompilerParams(vmem_limit_bytes=48 * 1024 * 1024),
        )(*whole, *args)

    def shift(value, steps):
        pairs = [(k, (k + steps) % n_fsdp) for k in range(n_fsdp)]
        return lax.ppermute(value, "fsdp", pairs)

    def ring(own):
        ahead, behind = [own], [own]
        for step in range(n_fsdp // 2):
            ahead.append(shift(ahead[-1], 1))
            if step < n_fsdp // 2 - 1:
                behind.append(shift(behind[-1], -1))
        return ahead + behind[:0:-1]

    def ring_whole(own):
        whole = unfilled(((n_fsdp,) + own.shape, BF))[0]
        whole = lax.dynamic_update_slice(whole, own[None], (0, 0, 0, 0))
        ahead, behind, count = own, own, 1
        for step in range(n_fsdp // 2):
            ahead = shift(ahead, 1)
            behind = shift(behind, -1) if step < n_fsdp // 2 - 1 else None
            for value in (behind, ahead):
                if value is not None:
                    whole = lax.dynamic_update_slice(whole, value[None], (count, 0, 0, 0))
                    count += 1
        return whole

    def near(value):
        return value.reshape(n_expert, n_fsdp, 8, value.shape[-1])

    def rows_of(*cols):
        return [((total, c), BF) for c in cols]

    spread, put, get, getz, near_get, near_getz = call(
        lambda *r: prep_body(micro, tok, cap, n_expert, n_fsdp, *r),
        [((8 * n_expert, wide), BF), ((tokens, 8 * n_expert), BF), ((2 * tokens, total), BF), ((top * tokens, total), BF)]
        + [((2 * tokens, 8 * n_expert), BF), ((top * tokens, 8 * n_expert), BF)],
        expert_ids,
        gates,
        acts.reshape(tokens, width),
    )
    loss_grad = out_grad.reshape(tokens, width)

    def merge(back, grad):
        return call(merge_body, [((tokens, width), BF)], get, back, grad)[0]

    def gate_of(value):
        return call(gate_body, [((1, micro, tok, top), F32)], getz, value)[0]

    def outer(x_rows, g_rows, da, db, hg):
        cost = pl.CostEstimate(flops=12 * total * width * hid, bytes_accessed=12 * total * half, transcendentals=0)
        shapes = [(w_gate.shape, BF), (w_up.shape, BF), (w_down.shape, BF)]
        return tuple(call(outer_body, shapes, x_rows, g_rows, da, db, hg, cost=cost))

    fsdp_now = lax.axis_index("fsdp")
    near_rows = 8 * n_expert
    blocks = (3, hid, width)
    def first():
        (send,) = call(
            place_both_body, [((n_expert, n_fsdp, 8, wide + half), BF)], spread, put, loss_grad
        )
        rows = exchange(send)
        out, da, db, z, hg, x_rows, g_rows = call_rows(
            both_body, rows_of(half, hid, hid, LANES, hid, half, half), [rows], [wd, wg, wu]
        )
        new = merge(exchange(out), loss_grad)
        unused = unfilled(
            ((total, hid), BF), ((total, hid), BF), ((total, hid), BF), ((near_rows, wide), BF), ((n_fsdp,) + blocks, BF)
        )
        return (new, z, g_rows, da, db), (x_rows, *unused[:3], hg), unused[3], unused[4]

    def spread_out(value):
        return exchange(call(fan_body, [((n_expert, n_fsdp, 8, wide), BF)], value)[0])

    def gather_rows():
        lent = lax.ppermute(spread, "segment", [(last - 1, 0)])
        whole = lax.cond(
            segment == 1,
            lambda: ring_whole(jnp.stack([wg.T, wu.T, wd])),
            lambda: unfilled(((n_fsdp,) + blocks, BF))[0],
        )
        far = whole[n_fsdp - 1, 0, 0, 0].astype(F32)
        rows = lax.cond(
            (segment == 0) | ((segment == 1) & (jnp.abs(far) < 1e30)),
            spread_out,
            lambda v: jnp.zeros((total, wide), BF),
            jnp.where(segment == 0, lent, spread),
        )
        handed = lax.ppermute(rows, "segment", [(0, last - 1)])
        rows = jnp.where(segment == last - 1, handed, rows)
        go = lax.ppermute(1.0 + 0.0 * rows[0, :8].astype(F32), "segment", [(1, 0)])
        rows = lax.cond(go[0] > 0.5, lambda v, e: spread_out(v), lambda v, e: e, spread, rows)
        slope, act, hidden, hg, x_rows = call_rows(
            forward_body, rows_of(hid, hid, hid, hid, half), [rows], [wg, wu], 2 * SMALL
        )
        plane = lax.dynamic_index_in_dim(near(rows), fsdp_now, 1, keepdims=False).reshape(near_rows, wide)
        state = unfilled(
            ((tokens, width), BF), ((total, LANES), BF), ((total, half), BF), ((total, hid), BF), ((total, hid), BF)
        )
        return tuple(state), (x_rows, slope, act, hidden, hg), plane, whole

    state, saved, plane, whole = lax.cond(segment == last, first, gather_rows)
    x_rows, slope, act, hidden, hg = saved

    def dispatch(grad):
        (send,) = call(place_body, [((n_expert, n_fsdp, 8, half), BF)], put, grad)
        return exchange(send)

    near_shape = ((n_fsdp, near_rows, hid), BF)

    near_slope, near_act, near_hid = lax.cond(
        segment == 1,
        lambda p, w: tuple(by_block(near_forward_body, [near_shape] * 3, [w], [p])),
        lambda *_: tuple(unfilled(near_shape, near_shape, near_shape)),
        plane,
        whole,
    )

    def exchange_near(value):
        cols = value.shape[-1]
        moved = lax.all_to_all(value.reshape(n_expert, 8, cols), "expert", 0, 0, tiled=True)
        return moved.reshape(near_rows, cols)

    gate_shape = ((1, micro, tok, top), F32)

    def relay(grad, new):
        (send,) = call(near_place_body, [((near_rows, half), BF)], put, grad)
        g_near = exchange_near(send)
        (out,) = by_block(
            near_back_body,
            [((near_rows, wide), BF)],
            [near_slope, near_act, near_hid, whole],
            [g_near],
            [(near_rows, half), (near_rows, half), (near_rows, LANES)],
        )
        back = exchange_near(out)
        new, gate = call(
            merge_gate_body, [((tokens, width), BF), gate_shape], near_get, near_getz, back, grad
        )
        return new, g_near, gate

    def relay_not(grad, new):
        return (new, *unfilled(((near_rows, half), BF), gate_shape))

    def middle(grad, state):
        g_rows = dispatch(grad)
        out, da, db, z = call_rows(
            back_body, rows_of(half, hid, hid, LANES), [g_rows, slope, act, hidden], [wd, wg, wu]
        )
        new = merge(exchange(out), grad)
        return new, z, g_rows, da, db

    def final(grad, state, done):
        g_rows = dispatch(grad)
        out, da, db = call_rows(
            back_body, rows_of(wide, hid, hid), [g_rows, slope, act, hidden], [wd, wg, wu]
        )
        back = exchange(out)
        grads = outer(x_rows, g_rows, da, db, hg)
        new, gate = call(
            merge_gate_body, [((tokens, width), BF), gate_shape], get, getz, back, grad
        )
        return (new, gate) + grads

    def collect(state, done):
        new, g_near, gate, _ = done
        g_all = jnp.zeros((n_expert, n_fsdp, 8, half), BF)
        for k, piece in enumerate(ring(g_near)):
            at = (0, (fsdp_now - k) % n_fsdp, 0, 0)
            g_all = lax.dynamic_update_slice(g_all, piece.reshape(n_expert, 1, 8, half), at)
        g_rows = g_all.reshape(total, half)
        da, db = call_rows(grad_body, rows_of(hid, hid), [g_rows, slope, act], [wd], SMALL)
        return gate, g_rows, da, db

    def settle(state, done):
        _, z, g_rows, da, db = state
        z = z + (0.0 * done[3][0]).astype(BF)
        return gate_of(exchange(z)), g_rows, da, db

    def finish(grad, state, done):
        gate, g_rows, da, db = lax.cond(segment == 1, collect, settle, state, done)
        return (done[0], gate) + outer(x_rows, g_rows, da, db, hg)

    def step_down(layer, new):
        return lax.ppermute(new, "segment", [(layer, layer - 1)])

    grad = step_down(last, state[0])
    for layer in range(last - 1, 1, -1):
        state = lax.cond(segment == layer, middle, lambda g, s: s, grad, state)
        grad = step_down(layer, state[0])
    new, g_near, gate = lax.cond(segment == 1, relay, relay_not, grad, state[0])
    grad = step_down(1, new)
    hold = lax.ppermute(1.0 + 0.0 * new[0, :8].astype(F32), "segment", [(1, last)])
    new, gate, grad_gate, grad_up, grad_down = lax.cond(
        segment == 0, final, finish, grad, state, (new, g_near, gate, hold)
    )
    return new.reshape(acts.shape), gate, grad_gate, grad_up, grad_down


def solution(mesh):
    in_specs = (
        P("segment", None, ("expert", "fsdp"), None),
        P(None, ("expert", "fsdp"), None),
        P("segment", None, ("expert", "fsdp"), None),
        P("segment", None, ("expert", "fsdp"), None),
        P("segment", "expert", None, "fsdp"),
        P("segment", "expert", None, "fsdp"),
        P("segment", "expert", "fsdp", None),
    )
    out_specs = (
        P("segment", None, ("expert", "fsdp"), None),
        P("segment", None, ("expert", "fsdp"), None),
        P("segment", "expert", None, "fsdp"),
        P("segment", "expert", None, "fsdp"),
        P("segment", "expert", "fsdp", None),
    )
    return jax.shard_map(local, mesh=mesh, in_specs=in_specs, out_specs=out_specs, check_vma=False)
```

```python
import jax
import jax.numpy as jnp
from jax import lax
from jax.experimental import pallas as pl
from jax.experimental.pallas import tpu as pltpu
from jax.sharding import PartitionSpec as P

BF = jnp.bfloat16
F32 = jnp.float32
NN = (((1,), (0,)), ((), ()))
NT = (((1,), (1,)), ((), ()))
TN = (((0,), (0,)), ((), ()))
LANES = 128
CHUNK = 512
SMALL = 128
ROUTE = ("expert", "fsdp")


def dot(a, b, dims):
    return lax.dot_general(a, b, dims, preferred_element_type=F32)


def iota(shape, dim):
    return lax.broadcasted_iota(jnp.int32, shape, dim)


def call(body, outs, *args, cost=None):
    return pl.pallas_call(
        body,
        out_shape=[jax.ShapeDtypeStruct(s, d) for s, d in outs],
        in_specs=[pl.BlockSpec(memory_space=pltpu.VMEM)] * len(args),
        out_specs=[pl.BlockSpec(memory_space=pltpu.VMEM)] * len(outs),
        compiler_params=pltpu.CompilerParams(vmem_limit_bytes=48 * 1024 * 1024),
        cost_estimate=cost,
    )(*args)


def call_rows(body, outs, streamed, whole, chunk=CHUNK):
    total = streamed[0].shape[0]
    by_rows = lambda shape: pl.BlockSpec((chunk, shape[1]), lambda i: (i, 0))
    return pl.pallas_call(
        body,
        grid=(total // chunk,),
        out_shape=[jax.ShapeDtypeStruct(s, d) for s, d in outs],
        in_specs=[by_rows(v.shape) for v in streamed] + [pl.BlockSpec(memory_space=pltpu.VMEM)] * len(whole),
        out_specs=[by_rows(s) for s, _ in outs],
        compiler_params=pltpu.CompilerParams(vmem_limit_bytes=48 * 1024 * 1024),
    )(*streamed, *whole)


def upper(rows, cols):
    return (iota((rows, cols), 0) % 8) >= 4


def place(routing, tokens):
    half = tokens.shape[1] // 2
    spread = dot(routing, tokens, TN)
    rows = spread.shape[0]
    return jnp.where(upper(rows, half), spread[:, half:], spread[:, :half]).astype(BF)


def prep_body(micro, tok, cap, n_expert, n_fsdp, ids_ref, gates_ref, x_ref, spread_ref, put_ref, get_ref, getz_ref, near_ref, nearz_ref):
    rows = micro * tok
    ids = jnp.concatenate([ids_ref[0, m] for m in range(micro)], axis=0)
    gates = jnp.concatenate([gates_ref[0, m].astype(F32) for m in range(micro)], axis=0)
    first, second = ids[:, 0:1], ids[:, 1:2]
    experts = iota((rows, LANES), 1)
    one, two = experts == first, experts == second
    counts = (one | two).astype(BF)
    r0, r1 = iota((rows, rows), 0), iota((rows, rows), 1)
    lower = ((r1 < r0) & (r1 // tok == r0 // tok)).astype(BF)
    before = dot(lower, counts, NN)
    place_of = iota((rows, 1), 0) // tok * cap
    slot_one = jnp.sum(jnp.where(one, before, 0.0), axis=1, keepdims=True).astype(jnp.int32) + place_of
    slot_two = jnp.sum(jnp.where(two, before, 0.0), axis=1, keepdims=True).astype(jnp.int32) + place_of
    cols = 8 * n_expert
    col = iota((rows, cols), 1)
    put_one = ((col // 8 == first) & (col % 4 == slot_one)).astype(F32)
    put_two = ((col // 8 == second) & (col % 4 == slot_two)).astype(F32)
    put = (put_one + put_two).astype(BF)
    put_ref[...] = put
    under = (col % 8) < 4
    near_ref[:rows] = jnp.where(under, put_one + put_two, 0.0).astype(BF)
    near_ref[rows:] = jnp.where(under, 0.0, put_one + put_two).astype(BF)
    nearz_ref[:rows] = jnp.where(under, put_one, 0.0).astype(BF)
    nearz_ref[rows:] = jnp.where(under, put_two, 0.0).astype(BF)
    put_gates = (put_one * gates[:, 0:1] + put_two * gates[:, 1:2]).astype(BF)
    half = x_ref.shape[1] // 2
    spread_ref[:, :half] = place(put, x_ref[...])
    spread_ref[:, half:] = dot(put_gates, jnp.ones((rows, LANES), BF), TN).astype(BF)
    total = 8 * n_expert * n_fsdp
    wide = iota((rows, total), 1)
    target = wide // (8 * n_fsdp)
    row = wide % 4
    low = (wide % 8) < 4
    hit_one = (target == first) & (row == slot_one)
    hit_two = (target == second) & (row == slot_two)
    hit = hit_one | hit_two
    get_ref[:rows] = jnp.where(hit & low, 1.0, 0.0).astype(BF)
    get_ref[rows:] = jnp.where(hit & ~low, 1.0, 0.0).astype(BF)
    getz_ref[:rows] = jnp.where(hit_one & low, 1.0, 0.0).astype(BF)
    getz_ref[rows:] = jnp.where(hit_two & low, 1.0, 0.0).astype(BF)


def fan(send_ref, value, at):
    n_expert, n_fsdp = send_ref.shape[:2]
    width = value.shape[1]
    send_ref[:, :, :, at : at + width] = jnp.broadcast_to(
        value.reshape(n_expert, 1, 8, width), (n_expert, n_fsdp, 8, width)
    )


def place_body(put_ref, g_ref, send_ref):
    fan(send_ref, place(put_ref[...], g_ref[...]), 0)


def fan_body(spread_ref, send_ref):
    fan(send_ref, spread_ref[...], 0)


def place_both_body(spread_ref, put_ref, g_ref, send_ref):
    fan(send_ref, spread_ref[...], 0)
    fan(send_ref, place(put_ref[...], g_ref[...]), spread_ref.shape[1])


def join(mine, other, mask):
    value = jnp.where(mask, other, mine)
    rows, cols = value.shape
    turned = pltpu.roll(value.reshape(rows // 8, 8, cols), 4, 1).reshape(rows, cols)
    return value + turned


def forward(x, c, wg_ref, wu_ref):
    half, hid = wg_ref.shape[0] // 2, wg_ref.shape[1]
    c = jnp.concatenate([c.astype(F32)] * (hid // LANES), axis=1)
    mask = upper(x.shape[0], hid)
    a = join(dot(x, wg_ref[:half, :], NN), dot(x, wg_ref[half:, :], NN), mask)
    b = join(dot(x, wu_ref[:half, :], NN), dot(x, wu_ref[half:, :], NN), mask)
    sig = jax.nn.sigmoid(a)
    s = a * sig
    h = s * b
    return c * (b * (sig * (1.0 + a * (1.0 - sig)))), c * s, h, (c * h).astype(BF)


def backward(g, slope, act, hidden, wd_ref, wg_ref, wu_ref):
    half, hid = wg_ref.shape[0] // 2, wg_ref.shape[1]
    rows = g.shape[0]
    q = join(dot(g, wd_ref[:, :half], NT), dot(g, wd_ref[:, half:], NT), upper(rows, hid))
    da = (q * slope).astype(BF)
    db = (q * act).astype(BF)
    low = dot(da, wg_ref[:half, :], NT) + dot(db, wu_ref[:half, :], NT)
    high = dot(da, wg_ref[half:, :], NT) + dot(db, wu_ref[half:, :], NT)
    out = jnp.where(upper(rows, half), high, low).astype(BF)
    z = jnp.sum(q * hidden, axis=1, keepdims=True)
    return da, db, out, jnp.broadcast_to(z, (rows, LANES)).astype(BF)


def forward_body(rows_ref, wg_ref, wu_ref, slope_ref, act_ref, hid_ref, hg_ref, x_ref):
    half = wg_ref.shape[0] // 2
    x = rows_ref[:, :half]
    x_ref[...] = x
    slope, act, hidden, hg_ref[...] = forward(x, rows_ref[:, half:], wg_ref, wu_ref)
    slope_ref[...] = slope.astype(BF)
    act_ref[...] = act.astype(BF)
    hid_ref[...] = hidden.astype(BF)


def back_body(rows_ref, slope_ref, act_ref, hid_ref, wd_ref, wg_ref, wu_ref, out_ref, da_ref, db_ref, *z_ref):
    half = wg_ref.shape[0] // 2
    da_ref[...], db_ref[...], out, z = backward(
        rows_ref[...],
        slope_ref[...].astype(F32),
        act_ref[...].astype(F32),
        hid_ref[...].astype(F32),
        wd_ref,
        wg_ref,
        wu_ref,
    )
    out_ref[:, :half] = out
    if z_ref:
        z_ref[0][...] = z
    else:
        out_ref[:, half:] = z


def grad_body(rows_ref, slope_ref, act_ref, wd_ref, da_ref, db_ref):
    half = wd_ref.shape[1] // 2
    g = rows_ref[...]
    mask = upper(g.shape[0], wd_ref.shape[0])
    q = join(dot(g, wd_ref[:, :half], NT), dot(g, wd_ref[:, half:], NT), mask)
    da_ref[...] = (q * slope_ref[...].astype(F32)).astype(BF)
    db_ref[...] = (q * act_ref[...].astype(F32)).astype(BF)


def both_body(rows_ref, wd_ref, wg_ref, wu_ref, out_ref, da_ref, db_ref, z_ref, hg_ref, x_ref, g_ref):
    half = wg_ref.shape[0] // 2
    x = rows_ref[:, :half]
    g = rows_ref[:, half + LANES :]
    x_ref[...] = x
    g_ref[...] = g
    slope, act, hidden, hg_ref[...] = forward(x, rows_ref[:, half : half + LANES], wg_ref, wu_ref)
    da_ref[...], db_ref[...], out_ref[...], z_ref[...] = backward(g, slope, act, hidden, wd_ref, wg_ref, wu_ref)


def nothing_body(*refs):
    pass


def near_place_body(put_ref, g_ref, send_ref):
    send_ref[...] = place(put_ref[...], g_ref[...])


def near_forward_body(rows_ref, w_ref, slope_ref, act_ref, hid_ref):
    half = w_ref.shape[3] // 2
    x, c = rows_ref[:, :half], rows_ref[:, half:]
    c = jnp.concatenate([c.astype(F32)] * (w_ref.shape[2] // LANES), axis=1)
    mask = upper(*c.shape)
    a = join(dot(x, w_ref[0, 0, :, :half], NT), dot(x, w_ref[0, 0, :, half:], NT), mask)
    b = join(dot(x, w_ref[0, 1, :, :half], NT), dot(x, w_ref[0, 1, :, half:], NT), mask)
    sig = jax.nn.sigmoid(a)
    s = a * sig
    slope_ref[0] = (c * (b * (sig * (1.0 + a * (1.0 - sig))))).astype(BF)
    act_ref[0] = (c * s).astype(BF)
    hid_ref[0] = (s * b).astype(BF)


def near_back_body(g_ref, slope_ref, act_ref, hid_ref, w_ref, out_ref, low_ref, high_ref, z_ref):
    half, hid = w_ref.shape[3] // 2, w_ref.shape[2]
    rows = g_ref.shape[0]
    block = pl.program_id(0)

    @pl.when(block == 0)
    def _():
        low_ref[...] = jnp.zeros_like(low_ref)
        high_ref[...] = jnp.zeros_like(high_ref)
        z_ref[...] = jnp.zeros_like(z_ref)

    g = g_ref[...]
    q = join(dot(g, w_ref[0, 2, :, :half], NT), dot(g, w_ref[0, 2, :, half:], NT), upper(rows, hid))
    da = (q * slope_ref[0].astype(F32)).astype(BF)
    db = (q * act_ref[0].astype(F32)).astype(BF)
    low_ref[...] += dot(da, w_ref[0, 0, :, :half], NN) + dot(db, w_ref[0, 1, :, :half], NN)
    high_ref[...] += dot(da, w_ref[0, 0, :, half:], NN) + dot(db, w_ref[0, 1, :, half:], NN)
    z = jnp.sum(q * hid_ref[0].astype(F32), axis=1, keepdims=True)
    z_ref[...] += jnp.broadcast_to(z, z_ref.shape)

    @pl.when(block == pl.num_programs(0) - 1)
    def _():
        out_ref[:, :half] = jnp.where(upper(rows, half), high_ref[...], low_ref[...]).astype(BF)
        out_ref[:, half:] = z_ref[...].astype(BF)


def merge_body(get_ref, back_ref, g_ref, new_ref):
    tokens, width = g_ref.shape
    half = width // 2
    summed = dot(get_ref[...], back_ref[:, :half], NN)
    g = g_ref[...].astype(F32)
    new_ref[:, :half] = (g[:, :half] + summed[:tokens]).astype(BF)
    new_ref[:, half:] = (g[:, half:] + summed[tokens:]).astype(BF)


def gate_body(getz_ref, z_ref, gate_ref):
    _, micro, tok, top = gate_ref.shape
    value = dot(getz_ref[...], z_ref[:, z_ref.shape[1] - LANES :], NN)
    for m in range(micro):
        parts = [value[(k * micro + m) * tok : (k * micro + m + 1) * tok, 0:1] for k in range(top)]
        gate_ref[0, m] = jnp.concatenate(parts, axis=1)


def merge_gate_body(get_ref, getz_ref, back_ref, g_ref, new_ref, gate_ref):
    merge_body(get_ref, back_ref, g_ref, new_ref)
    gate_body(getz_ref, back_ref, gate_ref)


def outer_body(x_ref, g_ref, da_ref, db_ref, hg_ref, gate_ref, up_ref, down_ref):
    total, half = x_ref.shape
    hid = da_ref.shape[1]
    mask = upper(total, hid)
    x = x_ref[...]
    for k in range(2):
        at = slice(k * half, (k + 1) * half)
        keep = mask if k else ~mask
        only = lambda ref: jnp.where(keep, ref[...].astype(F32), 0.0).astype(BF)
        gate_ref[0, 0, at, :] = dot(x, only(da_ref), TN).astype(BF)
        up_ref[0, 0, at, :] = dot(x, only(db_ref), TN).astype(BF)
        down_ref[0, 0, :, at] = dot(only(hg_ref), g_ref[...], TN).astype(BF)


def local(acts, out_grad, expert_ids, gates, w_gate, w_up, w_down):
    segments = lax.axis_size("segment")
    segment = lax.axis_index("segment")
    n_expert = lax.axis_size("expert")
    n_fsdp = lax.axis_size("fsdp")
    _, micro, tok, width = acts.shape
    top = expert_ids.shape[3]
    cap = top * tok // n_expert
    tokens = micro * tok
    half = width // 2
    wide = half + LANES
    wg, wu, wd = w_gate[0, 0], w_up[0, 0], w_down[0, 0]
    hid = wg.shape[1]
    total = 8 * n_expert * n_fsdp
    sources = n_expert * n_fsdp
    last = segments - 1

    def exchange(value):
        cols = value.shape[-1]
        moved = lax.all_to_all(value.reshape(sources, 8, cols), ROUTE, 0, 0, tiled=True)
        return moved.reshape(total, cols)

    def unfilled(*shapes):
        return pl.pallas_call(
            nothing_body,
            out_shape=[jax.ShapeDtypeStruct(s, d) for s, d in shapes],
            out_specs=[pl.BlockSpec(memory_space=pl.ANY)] * len(shapes),
        )()

    def by_block(body, outs, args, whole, scratch=(), first=None):
        one = lambda v: pl.BlockSpec((1,) + v[1:], lambda i: (i,) + (0,) * (len(v) - 1))
        stay = lambda v: pl.BlockSpec(v, lambda i: (0,) * len(v))
        return pl.pallas_call(
            body,
            grid=(n_fsdp,),
            out_shape=[jax.ShapeDtypeStruct(v, d) for v, d in outs],
            in_specs=[stay(v.shape) for v in whole]
            + [one(v.shape if first is None else (v.shape[0], first) + v.shape[2:]) for v in args],
            out_specs=[one(v) if len(v) > 2 else stay(v) for v, _ in outs],
            scratch_shapes=[pltpu.VMEM(v, F32) for v in scratch],
            compiler_params=pltpu.CompilerParams(vmem_limit_bytes=48 * 1024 * 1024),
        )(*whole, *args)

    def shift(value, steps):
        pairs = [(k, (k + steps) % n_fsdp) for k in range(n_fsdp)]
        return lax.ppermute(value, "fsdp", pairs)

    def ring(own):
        ahead, behind = [own], [own]
        for step in range(n_fsdp // 2):
            ahead.append(shift(ahead[-1], 1))
            if step < n_fsdp // 2 - 1:
                behind.append(shift(behind[-1], -1))
        return ahead + behind[:0:-1]

    def ring_whole(own):
        whole = unfilled(((n_fsdp,) + own.shape, BF))[0]
        whole = lax.dynamic_update_slice(whole, own[None], (0, 0, 0, 0))
        ahead, behind, count = own, own, 1
        for _ in range(n_fsdp // 2 - 1):
            ahead, behind = shift(ahead, 1), shift(behind, -1)
            for value in (ahead, behind):
                whole = lax.dynamic_update_slice(whole, value[None], (count, 0, 0, 0))
                count += 1
        cut = own.shape[1] // 2
        one, two = shift(ahead[:, :cut], 1), shift(behind[:, cut:], -1)
        whole = lax.dynamic_update_slice(whole, one[None], (count, 0, 0, 0))
        whole = lax.dynamic_update_slice(whole, two[None], (count, 0, cut, 0))
        return whole

    def near(value):
        return value.reshape(n_expert, n_fsdp, 8, value.shape[-1])

    def rows_of(*cols):
        return [((total, c), BF) for c in cols]

    spread, put, get, getz, near_get, near_getz = call(
        lambda *r: prep_body(micro, tok, cap, n_expert, n_fsdp, *r),
        [((8 * n_expert, wide), BF), ((tokens, 8 * n_expert), BF), ((2 * tokens, total), BF), ((top * tokens, total), BF)]
        + [((2 * tokens, 8 * n_expert), BF), ((top * tokens, 8 * n_expert), BF)],
        expert_ids,
        gates,
        acts.reshape(tokens, width),
    )
    loss_grad = out_grad.reshape(tokens, width)

    def merge(back, grad):
        return call(merge_body, [((tokens, width), BF)], get, back, grad)[0]

    def gate_of(value):
        return call(gate_body, [((1, micro, tok, top), F32)], getz, value)[0]

    def outer(x_rows, g_rows, da, db, hg):
        cost = pl.CostEstimate(flops=12 * total * width * hid, bytes_accessed=12 * total * half, transcendentals=0)
        shapes = [(w_gate.shape, BF), (w_up.shape, BF), (w_down.shape, BF)]
        return tuple(call(outer_body, shapes, x_rows, g_rows, da, db, hg, cost=cost))

    fsdp_now = lax.axis_index("fsdp")
    near_rows = 8 * n_expert
    blocks = (3, hid, width)
    def first():
        (send,) = call(
            place_both_body, [((n_expert, n_fsdp, 8, wide + half), BF)], spread, put, loss_grad
        )
        rows = exchange(send)
        out, da, db, z, hg, x_rows, g_rows = call_rows(
            both_body, rows_of(half, hid, hid, LANES, hid, half, half), [rows], [wd, wg, wu]
        )
        new = merge(exchange(out), loss_grad)
        unused = unfilled(
            ((total, hid), BF), ((total, hid), BF), ((total, hid), BF), ((near_rows, wide), BF), ((n_fsdp,) + blocks, BF)
        )
        return (new, z, g_rows, da, db), (x_rows, *unused[:3], hg), unused[3], unused[4]

    def spread_out(value):
        return exchange(call(fan_body, [((n_expert, n_fsdp, 8, wide), BF)], value)[0])

    def gather_rows():
        lent = lax.ppermute(spread, "segment", [(last - 1, 0)])
        whole = lax.cond(
            segment == 1,
            lambda: ring_whole(jnp.stack([wg.T, wu.T, wd])),
            lambda: unfilled(((n_fsdp,) + blocks, BF))[0],
        )
        far = whole[n_fsdp - 1, 0, 0, 0].astype(F32)
        rows = lax.cond(
            (segment == 0) | ((segment == 1) & (jnp.abs(far) < 1e30)),
            spread_out,
            lambda v: jnp.zeros((total, wide), BF),
            jnp.where(segment == 0, lent, spread),
        )
        handed = lax.ppermute(rows, "segment", [(0, last - 1)])
        go = lax.ppermute(1.0 + 0.0 * rows[0, :8].astype(F32), "segment", [(1, 0)])
        rows = lax.switch(
            jnp.where(segment == last - 1, 2, jnp.where(go[0] > 0.5, 0, 1)),
            (lambda v, e, h: spread_out(v), lambda v, e, h: e, lambda v, e, h: h),
            spread, rows, handed,
        )
        slope, act, hidden, hg, x_rows = call_rows(
            forward_body, rows_of(hid, hid, hid, hid, half), [rows], [wg, wu], 2 * SMALL
        )
        plane = lax.dynamic_index_in_dim(near(rows), fsdp_now, 1, keepdims=False).reshape(near_rows, wide)
        state = unfilled(
            ((tokens, width), BF), ((total, LANES), BF), ((total, half), BF), ((total, hid), BF), ((total, hid), BF)
        )
        return tuple(state), (x_rows, slope, act, hidden, hg), plane, whole

    state, saved, plane, whole = lax.cond(segment == last, first, gather_rows)
    x_rows, slope, act, hidden, hg = saved

    def dispatch(grad):
        (send,) = call(place_body, [((n_expert, n_fsdp, 8, half), BF)], put, grad)
        return exchange(send)

    near_shape = ((n_fsdp, near_rows, hid), BF)

    near_slope, near_act, near_hid = lax.cond(
        segment == 1,
        lambda p, w: tuple(by_block(near_forward_body, [near_shape] * 3, [w], [p], first=2)),
        lambda *_: tuple(unfilled(near_shape, near_shape, near_shape)),
        plane,
        whole,
    )

    def exchange_near(value):
        cols = value.shape[-1]
        moved = lax.all_to_all(value.reshape(n_expert, 8, cols), "expert", 0, 0, tiled=True)
        return moved.reshape(near_rows, cols)

    gate_shape = ((1, micro, tok, top), F32)

    def relay(grad, new):
        (send,) = call(near_place_body, [((near_rows, half), BF)], put, grad)
        g_near = exchange_near(send)
        (out,) = by_block(
            near_back_body,
            [((near_rows, wide), BF)],
            [near_slope, near_act, near_hid, whole],
            [g_near],
            [(near_rows, half), (near_rows, half), (near_rows, LANES)],
        )
        back = exchange_near(out)
        new, gate = call(
            merge_gate_body, [((tokens, width), BF), gate_shape], near_get, near_getz, back, grad
        )
        return new, g_near, gate

    def relay_not(grad, new):
        return (new, *unfilled(((near_rows, half), BF), gate_shape))

    def middle(grad, state):
        g_rows = dispatch(grad)
        out, da, db, z = call_rows(
            back_body, rows_of(half, hid, hid, LANES), [g_rows, slope, act, hidden], [wd, wg, wu]
        )
        new = merge(exchange(out), grad)
        return new, z, g_rows, da, db

    def final(grad, state, done):
        g_rows = dispatch(grad)
        out, da, db = call_rows(
            back_body, rows_of(wide, hid, hid), [g_rows, slope, act, hidden], [wd, wg, wu]
        )
        back = exchange(out)
        grads = outer(x_rows, g_rows, da, db, hg)
        new, gate = call(
            merge_gate_body, [((tokens, width), BF), gate_shape], get, getz, back, grad
        )
        return (new, gate) + grads

    def collect(state, done):
        new, g_near, gate, _ = done
        g_all = jnp.zeros((n_expert, n_fsdp, 8, half), BF)
        for k, piece in enumerate(ring(g_near)):
            at = (0, (fsdp_now - k) % n_fsdp, 0, 0)
            g_all = lax.dynamic_update_slice(g_all, piece.reshape(n_expert, 1, 8, half), at)
        g_rows = g_all.reshape(total, half)
        da, db = call_rows(grad_body, rows_of(hid, hid), [g_rows, slope, act], [wd], SMALL)
        return gate, g_rows, da, db

    def settle(state, done):
        _, z, g_rows, da, db = state
        z = z + (0.0 * done[3][0]).astype(BF)
        return gate_of(exchange(z)), g_rows, da, db

    def finish(grad, state, done):
        gate, g_rows, da, db = lax.cond(segment == 1, collect, settle, state, done)
        return (done[0], gate) + outer(x_rows, g_rows, da, db, hg)

    def step_down(layer, new):
        return lax.ppermute(new, "segment", [(layer, layer - 1)])

    grad = step_down(last, state[0])
    for layer in range(last - 1, 1, -1):
        state = lax.cond(segment == layer, middle, lambda g, s: s, grad, state)
        grad = step_down(layer, state[0])
    new, g_near, gate = lax.cond(segment == 1, relay, relay_not, grad, state[0])
    grad = step_down(1, new)
    hold = lax.ppermute(1.0 + 0.0 * new[0, :8].astype(F32), "segment", [(1, last)])
    new, gate, grad_gate, grad_up, grad_down = lax.cond(
        segment == 0, final, finish, grad, state, (new, g_near, gate, hold)
    )
    return new.reshape(acts.shape), gate, grad_gate, grad_up, grad_down


def solution(mesh):
    in_specs = (
        P("segment", None, ("expert", "fsdp"), None),
        P(None, ("expert", "fsdp"), None),
        P("segment", None, ("expert", "fsdp"), None),
        P("segment", None, ("expert", "fsdp"), None),
        P("segment", "expert", None, "fsdp"),
        P("segment", "expert", None, "fsdp"),
        P("segment", "expert", "fsdp", None),
    )
    out_specs = (
        P("segment", None, ("expert", "fsdp"), None),
        P("segment", None, ("expert", "fsdp"), None),
        P("segment", "expert", None, "fsdp"),
        P("segment", "expert", None, "fsdp"),
        P("segment", "expert", "fsdp", None),
    )
    return jax.shard_map(local, mesh=mesh, in_specs=in_specs, out_specs=out_specs, check_vma=False)
```

```python
import jax
import jax.numpy as jnp
from jax import lax
from jax.experimental import pallas as pl
from jax.experimental.pallas import tpu as pltpu
from jax.sharding import PartitionSpec as P

BF = jnp.bfloat16
F32 = jnp.float32
NN = (((1,), (0,)), ((), ()))
NT = (((1,), (1,)), ((), ()))
TN = (((0,), (0,)), ((), ()))
LANES = 128
CHUNK = 512
SMALL = 128
ROUTE = ("expert", "fsdp")


def dot(a, b, dims):
    return lax.dot_general(a, b, dims, preferred_element_type=F32)


def iota(shape, dim):
    return lax.broadcasted_iota(jnp.int32, shape, dim)


def call(body, outs, *args, cost=None):
    return pl.pallas_call(
        body,
        out_shape=[jax.ShapeDtypeStruct(s, d) for s, d in outs],
        in_specs=[pl.BlockSpec(memory_space=pltpu.VMEM)] * len(args),
        out_specs=[pl.BlockSpec(memory_space=pltpu.VMEM)] * len(outs),
        compiler_params=pltpu.CompilerParams(vmem_limit_bytes=48 * 1024 * 1024),
        cost_estimate=cost,
    )(*args)


def call_rows(body, outs, streamed, whole, chunk=CHUNK):
    total = streamed[0].shape[0]
    by_rows = lambda shape: pl.BlockSpec((chunk, shape[1]), lambda i: (i, 0))
    return pl.pallas_call(
        body,
        grid=(total // chunk,),
        out_shape=[jax.ShapeDtypeStruct(s, d) for s, d in outs],
        in_specs=[by_rows(v.shape) for v in streamed] + [pl.BlockSpec(memory_space=pltpu.VMEM)] * len(whole),
        out_specs=[by_rows(s) for s, _ in outs],
        compiler_params=pltpu.CompilerParams(vmem_limit_bytes=48 * 1024 * 1024),
    )(*streamed, *whole)


def upper(rows, cols):
    return (iota((rows, cols), 0) % 8) >= 4


def place(routing, tokens):
    half = tokens.shape[1] // 2
    spread = dot(routing, tokens, TN)
    rows = spread.shape[0]
    return jnp.where(upper(rows, half), spread[:, half:], spread[:, :half]).astype(BF)


def prep_body(micro, tok, cap, n_expert, n_fsdp, ids_ref, gates_ref, x_ref, spread_ref, put_ref, get_ref, getz_ref, near_ref, nearz_ref):
    rows = micro * tok
    ids = jnp.concatenate([ids_ref[0, m] for m in range(micro)], axis=0)
    gates = jnp.concatenate([gates_ref[0, m].astype(F32) for m in range(micro)], axis=0)
    first, second = ids[:, 0:1], ids[:, 1:2]
    experts = iota((rows, LANES), 1)
    one, two = experts == first, experts == second
    counts = (one | two).astype(BF)
    r0, r1 = iota((rows, rows), 0), iota((rows, rows), 1)
    lower = ((r1 < r0) & (r1 // tok == r0 // tok)).astype(BF)
    before = dot(lower, counts, NN)
    place_of = iota((rows, 1), 0) // tok * cap
    slot_one = jnp.sum(jnp.where(one, before, 0.0), axis=1, keepdims=True).astype(jnp.int32) + place_of
    slot_two = jnp.sum(jnp.where(two, before, 0.0), axis=1, keepdims=True).astype(jnp.int32) + place_of
    cols = 8 * n_expert
    col = iota((rows, cols), 1)
    put_one = ((col // 8 == first) & (col % 4 == slot_one)).astype(F32)
    put_two = ((col // 8 == second) & (col % 4 == slot_two)).astype(F32)
    put = (put_one + put_two).astype(BF)
    put_ref[...] = put
    under = (col % 8) < 4
    near_ref[:rows] = jnp.where(under, put_one + put_two, 0.0).astype(BF)
    near_ref[rows:] = jnp.where(under, 0.0, put_one + put_two).astype(BF)
    nearz_ref[:rows] = jnp.where(under, put_one, 0.0).astype(BF)
    nearz_ref[rows:] = jnp.where(under, put_two, 0.0).astype(BF)
    put_gates = (put_one * gates[:, 0:1] + put_two * gates[:, 1:2]).astype(BF)
    half = x_ref.shape[1] // 2
    spread_ref[:, :half] = place(put, x_ref[...])
    spread_ref[:, half:] = dot(put_gates, jnp.ones((rows, LANES), BF), TN).astype(BF)
    total = 8 * n_expert * n_fsdp
    wide = iota((rows, total), 1)
    target = wide // (8 * n_fsdp)
    row = wide % 4
    low = (wide % 8) < 4
    hit_one = (target == first) & (row == slot_one)
    hit_two = (target == second) & (row == slot_two)
    hit = hit_one | hit_two
    get_ref[:rows] = jnp.where(hit & low, 1.0, 0.0).astype(BF)
    get_ref[rows:] = jnp.where(hit & ~low, 1.0, 0.0).astype(BF)
    getz_ref[:rows] = jnp.where(hit_one & low, 1.0, 0.0).astype(BF)
    getz_ref[rows:] = jnp.where(hit_two & low, 1.0, 0.0).astype(BF)


def fan(send_ref, value, at):
    n_expert, n_fsdp = send_ref.shape[:2]
    width = value.shape[1]
    send_ref[:, :, :, at : at + width] = jnp.broadcast_to(
        value.reshape(n_expert, 1, 8, width), (n_expert, n_fsdp, 8, width)
    )


def place_body(put_ref, g_ref, send_ref):
    fan(send_ref, place(put_ref[...], g_ref[...]), 0)


def fan_body(spread_ref, send_ref):
    fan(send_ref, spread_ref[...], 0)


def place_both_body(spread_ref, put_ref, g_ref, send_ref):
    fan(send_ref, spread_ref[...], 0)
    fan(send_ref, place(put_ref[...], g_ref[...]), spread_ref.shape[1])


def join(mine, other, mask):
    value = jnp.where(mask, other, mine)
    rows, cols = value.shape
    turned = pltpu.roll(value.reshape(rows // 8, 8, cols), 4, 1).reshape(rows, cols)
    return value + turned


def forward(x, c, wg_ref, wu_ref):
    half, hid = wg_ref.shape[0] // 2, wg_ref.shape[1]
    c = jnp.concatenate([c.astype(F32)] * (hid // LANES), axis=1)
    mask = upper(x.shape[0], hid)
    a = join(dot(x, wg_ref[:half, :], NN), dot(x, wg_ref[half:, :], NN), mask)
    b = join(dot(x, wu_ref[:half, :], NN), dot(x, wu_ref[half:, :], NN), mask)
    sig = jax.nn.sigmoid(a)
    s = a * sig
    h = s * b
    return c * (b * (sig * (1.0 + a * (1.0 - sig)))), c * s, h, (c * h).astype(BF)


def backward(g, slope, act, hidden, wd_ref, wg_ref, wu_ref):
    half, hid = wg_ref.shape[0] // 2, wg_ref.shape[1]
    rows = g.shape[0]
    q = join(dot(g, wd_ref[:, :half], NT), dot(g, wd_ref[:, half:], NT), upper(rows, hid))
    da = (q * slope).astype(BF)
    db = (q * act).astype(BF)
    low = dot(da, wg_ref[:half, :], NT) + dot(db, wu_ref[:half, :], NT)
    high = dot(da, wg_ref[half:, :], NT) + dot(db, wu_ref[half:, :], NT)
    out = jnp.where(upper(rows, half), high, low).astype(BF)
    z = jnp.sum(q * hidden, axis=1, keepdims=True)
    return da, db, out, jnp.broadcast_to(z, (rows, LANES)).astype(BF)


def forward_body(rows_ref, wg_ref, wu_ref, slope_ref, act_ref, hid_ref, hg_ref, x_ref):
    half = wg_ref.shape[0] // 2
    x = rows_ref[:, :half]
    x_ref[...] = x
    slope, act, hidden, hg_ref[...] = forward(x, rows_ref[:, half:], wg_ref, wu_ref)
    slope_ref[...] = slope.astype(BF)
    act_ref[...] = act.astype(BF)
    hid_ref[...] = hidden.astype(BF)


def back_body(rows_ref, slope_ref, act_ref, hid_ref, wd_ref, wg_ref, wu_ref, out_ref, da_ref, db_ref, *z_ref):
    half = wg_ref.shape[0] // 2
    da_ref[...], db_ref[...], out, z = backward(
        rows_ref[...],
        slope_ref[...].astype(F32),
        act_ref[...].astype(F32),
        hid_ref[...].astype(F32),
        wd_ref,
        wg_ref,
        wu_ref,
    )
    out_ref[:, :half] = out
    if z_ref:
        z_ref[0][...] = z
    else:
        out_ref[:, half:] = z


def grad_body(rows_ref, slope_ref, act_ref, wd_ref, da_ref, db_ref):
    half = wd_ref.shape[1] // 2
    g = rows_ref[...]
    mask = upper(g.shape[0], wd_ref.shape[0])
    q = join(dot(g, wd_ref[:, :half], NT), dot(g, wd_ref[:, half:], NT), mask)
    da_ref[...] = (q * slope_ref[...].astype(F32)).astype(BF)
    db_ref[...] = (q * act_ref[...].astype(F32)).astype(BF)


def both_body(rows_ref, wd_ref, wg_ref, wu_ref, out_ref, da_ref, db_ref, z_ref, hg_ref, x_ref, g_ref):
    half = wg_ref.shape[0] // 2
    x = rows_ref[:, :half]
    g = rows_ref[:, half + LANES :]
    x_ref[...] = x
    g_ref[...] = g
    slope, act, hidden, hg_ref[...] = forward(x, rows_ref[:, half : half + LANES], wg_ref, wu_ref)
    da_ref[...], db_ref[...], out_ref[...], z_ref[...] = backward(g, slope, act, hidden, wd_ref, wg_ref, wu_ref)


def nothing_body(*refs):
    pass


def near_place_body(put_ref, g_ref, send_ref):
    send_ref[...] = place(put_ref[...], g_ref[...])


def near_forward_body(rows_ref, w_ref, slope_ref, act_ref, hid_ref):
    half = w_ref.shape[3] // 2
    x, c = rows_ref[:, :half], rows_ref[:, half:]
    c = jnp.concatenate([c.astype(F32)] * (w_ref.shape[2] // LANES), axis=1)
    mask = upper(*c.shape)
    a = join(dot(x, w_ref[0, 0, :, :half], NT), dot(x, w_ref[0, 0, :, half:], NT), mask)
    b = join(dot(x, w_ref[0, 1, :, :half], NT), dot(x, w_ref[0, 1, :, half:], NT), mask)
    sig = jax.nn.sigmoid(a)
    s = a * sig
    slope_ref[0] = (c * (b * (sig * (1.0 + a * (1.0 - sig))))).astype(BF)
    act_ref[0] = (c * s).astype(BF)
    hid_ref[0] = (s * b).astype(BF)


def near_back_body(g_ref, slope_ref, act_ref, hid_ref, w_ref, out_ref, low_ref, high_ref, z_ref):
    half, hid = w_ref.shape[3] // 2, w_ref.shape[2]
    rows = g_ref.shape[0]
    block = pl.program_id(0)

    @pl.when(block == 0)
    def _():
        low_ref[...] = jnp.zeros_like(low_ref)
        high_ref[...] = jnp.zeros_like(high_ref)
        z_ref[...] = jnp.zeros_like(z_ref)

    g = g_ref[...]
    q = join(dot(g, w_ref[0, 2, :, :half], NT), dot(g, w_ref[0, 2, :, half:], NT), upper(rows, hid))
    da = (q * slope_ref[0].astype(F32)).astype(BF)
    db = (q * act_ref[0].astype(F32)).astype(BF)
    low_ref[...] += dot(da, w_ref[0, 0, :, :half], NN) + dot(db, w_ref[0, 1, :, :half], NN)
    high_ref[...] += dot(da, w_ref[0, 0, :, half:], NN) + dot(db, w_ref[0, 1, :, half:], NN)
    z = jnp.sum(q * hid_ref[0].astype(F32), axis=1, keepdims=True)
    z_ref[...] += jnp.broadcast_to(z, z_ref.shape)

    @pl.when(block == pl.num_programs(0) - 1)
    def _():
        out_ref[:, :half] = jnp.where(upper(rows, half), high_ref[...], low_ref[...]).astype(BF)
        out_ref[:, half:] = z_ref[...].astype(BF)


def merge_body(get_ref, back_ref, g_ref, new_ref):
    tokens, width = g_ref.shape
    half = width // 2
    summed = dot(get_ref[...], back_ref[:, :half], NN)
    g = g_ref[...].astype(F32)
    new_ref[:, :half] = (g[:, :half] + summed[:tokens]).astype(BF)
    new_ref[:, half:] = (g[:, half:] + summed[tokens:]).astype(BF)


def gate_body(getz_ref, z_ref, gate_ref):
    _, micro, tok, top = gate_ref.shape
    value = dot(getz_ref[...], z_ref[:, z_ref.shape[1] - LANES :], NN)
    for m in range(micro):
        parts = [value[(k * micro + m) * tok : (k * micro + m + 1) * tok, 0:1] for k in range(top)]
        gate_ref[0, m] = jnp.concatenate(parts, axis=1)


def merge_gate_body(get_ref, getz_ref, back_ref, g_ref, new_ref, gate_ref):
    merge_body(get_ref, back_ref, g_ref, new_ref)
    gate_body(getz_ref, back_ref, gate_ref)


def outer_body(x_ref, g_ref, da_ref, db_ref, hg_ref, gate_ref, up_ref, down_ref):
    total, half = x_ref.shape
    hid = da_ref.shape[1]
    mask = upper(total, hid)
    x = x_ref[...]
    for k in range(2):
        at = slice(k * half, (k + 1) * half)
        keep = mask if k else ~mask
        only = lambda ref: jnp.where(keep, ref[...].astype(F32), 0.0).astype(BF)
        gate_ref[0, 0, at, :] = dot(x, only(da_ref), TN).astype(BF)
        up_ref[0, 0, at, :] = dot(x, only(db_ref), TN).astype(BF)
        down_ref[0, 0, :, at] = dot(only(hg_ref), g_ref[...], TN).astype(BF)


def local(acts, out_grad, expert_ids, gates, w_gate, w_up, w_down):
    segments = lax.axis_size("segment")
    segment = lax.axis_index("segment")
    n_expert = lax.axis_size("expert")
    n_fsdp = lax.axis_size("fsdp")
    _, micro, tok, width = acts.shape
    top = expert_ids.shape[3]
    cap = top * tok // n_expert
    tokens = micro * tok
    half = width // 2
    wide = half + LANES
    wg, wu, wd = w_gate[0, 0], w_up[0, 0], w_down[0, 0]
    hid = wg.shape[1]
    total = 8 * n_expert * n_fsdp
    sources = n_expert * n_fsdp
    last = segments - 1

    def exchange(value):
        cols = value.shape[-1]
        moved = lax.all_to_all(value.reshape(sources, 8, cols), ROUTE, 0, 0, tiled=True)
        return moved.reshape(total, cols)

    def unfilled(*shapes):
        return pl.pallas_call(
            nothing_body,
            out_shape=[jax.ShapeDtypeStruct(s, d) for s, d in shapes],
            out_specs=[pl.BlockSpec(memory_space=pl.ANY)] * len(shapes),
        )()

    def by_block(body, outs, args, whole, scratch=(), first=None):
        one = lambda v: pl.BlockSpec((1,) + v[1:], lambda i: (i,) + (0,) * (len(v) - 1))
        stay = lambda v: pl.BlockSpec(v, lambda i: (0,) * len(v))
        return pl.pallas_call(
            body,
            grid=(n_fsdp,),
            out_shape=[jax.ShapeDtypeStruct(v, d) for v, d in outs],
            in_specs=[stay(v.shape) for v in whole]
            + [one(v.shape if first is None else (v.shape[0], first) + v.shape[2:]) for v in args],
            out_specs=[one(v) if len(v) > 2 else stay(v) for v, _ in outs],
            scratch_shapes=[pltpu.VMEM(v, F32) for v in scratch],
            compiler_params=pltpu.CompilerParams(vmem_limit_bytes=48 * 1024 * 1024),
        )(*whole, *args)

    def shift(value, steps):
        pairs = [(k, (k + steps) % n_fsdp) for k in range(n_fsdp)]
        return lax.ppermute(value, "fsdp", pairs)

    def ring(own):
        ahead, behind = [own], [own]
        for step in range(n_fsdp // 2):
            ahead.append(shift(ahead[-1], 1))
            if step < n_fsdp // 2 - 1:
                behind.append(shift(behind[-1], -1))
        return ahead + behind[:0:-1]

    def ring_whole(own):
        whole = unfilled(((n_fsdp,) + own.shape, BF))[0]
        whole = lax.dynamic_update_slice(whole, own[None], (0, 0, 0, 0))
        ahead, behind, count = own, own, 1
        for _ in range(n_fsdp // 2 - 1):
            ahead, behind = shift(ahead, 1), shift(behind, -1)
            for value in (ahead, behind):
                whole = lax.dynamic_update_slice(whole, value[None], (count, 0, 0, 0))
                count += 1
        cut = own.shape[1] // 2
        one, two = shift(ahead[:, :cut], 1), shift(behind[:, cut:], -1)
        whole = lax.dynamic_update_slice(whole, one[None], (count, 0, 0, 0))
        whole = lax.dynamic_update_slice(whole, two[None], (count, 0, cut, 0))
        return whole

    def near(value):
        return value.reshape(n_expert, n_fsdp, 8, value.shape[-1])

    def rows_of(*cols):
        return [((total, c), BF) for c in cols]

    spread, put, get, getz, near_get, near_getz = call(
        lambda *r: prep_body(micro, tok, cap, n_expert, n_fsdp, *r),
        [((8 * n_expert, wide), BF), ((tokens, 8 * n_expert), BF), ((2 * tokens, total), BF), ((top * tokens, total), BF)]
        + [((2 * tokens, 8 * n_expert), BF), ((top * tokens, 8 * n_expert), BF)],
        expert_ids,
        gates,
        acts.reshape(tokens, width),
    )
    loss_grad = out_grad.reshape(tokens, width)

    def merge(back, grad):
        return call(merge_body, [((tokens, width), BF)], get, back, grad)[0]

    def gate_of(value):
        return call(gate_body, [((1, micro, tok, top), F32)], getz, value)[0]

    def outer(x_rows, g_rows, da, db, hg):
        cost = pl.CostEstimate(flops=12 * total * width * hid, bytes_accessed=12 * total * half, transcendentals=0)
        shapes = [(w_gate.shape, BF), (w_up.shape, BF), (w_down.shape, BF)]
        return tuple(call(outer_body, shapes, x_rows, g_rows, da, db, hg, cost=cost))

    fsdp_now = lax.axis_index("fsdp")
    near_rows = 8 * n_expert
    blocks = (3, hid, width)
    def first():
        (send,) = call(
            place_both_body, [((n_expert, n_fsdp, 8, wide + half), BF)], spread, put, loss_grad
        )
        rows = exchange(send)
        out, da, db, z, hg, x_rows, g_rows = call_rows(
            both_body, rows_of(half, hid, hid, LANES, hid, half, half), [rows], [wd, wg, wu]
        )
        new = merge(exchange(out), loss_grad)
        unused = unfilled(
            ((total, hid), BF), ((total, hid), BF), ((total, hid), BF), ((near_rows, wide), BF), ((n_fsdp,) + blocks, BF)
        )
        return (new, z, g_rows, da, db), (x_rows, *unused[:3], hg), unused[3], unused[4]

    def spread_out(value):
        return exchange(call(fan_body, [((n_expert, n_fsdp, 8, wide), BF)], value)[0])

    def gather_rows():
        nil = lambda v: 0.0 * v[(0,) * v.ndim]
        lent_one = lax.ppermute(spread, "segment", [(1, 0)])
        lent_two = lax.ppermute(spread, "segment", [(last - 1, 0)])
        whole = lax.cond(
            segment == 1,
            lambda: ring_whole(jnp.stack([wg.T, wu.T, wd]) + nil(lent_one).astype(BF)),
            lambda: unfilled(((n_fsdp,) + blocks, BF))[0],
        )

        def on_zero(value):
            return lax.cond(segment == 0, spread_out, lambda v: jnp.zeros((total, wide), BF), value)

        rows_two = on_zero(lent_two + nil(lent_one).astype(BF))
        handed_two = lax.ppermute(rows_two, "segment", [(0, last - 1)])
        rows_one = on_zero(lent_one + nil(handed_two).astype(BF))
        handed_one = lax.ppermute(rows_one, "segment", [(0, 1)])
        rows = on_zero(spread + nil(handed_one).astype(BF))
        rows = lax.switch(
            jnp.minimum(segment, 2),
            (lambda a, b, c: a, lambda a, b, c: b, lambda a, b, c: c),
            rows, handed_one, handed_two,
        )
        slope, act, hidden, hg, x_rows = call_rows(
            forward_body, rows_of(hid, hid, hid, hid, half), [rows], [wg, wu], 2 * SMALL
        )
        plane = lax.dynamic_index_in_dim(near(rows), fsdp_now, 1, keepdims=False).reshape(near_rows, wide)
        state = unfilled(
            ((tokens, width), BF), ((total, LANES), BF), ((total, half), BF), ((total, hid), BF), ((total, hid), BF)
        )
        return tuple(state), (x_rows, slope, act, hidden, hg), plane, whole

    state, saved, plane, whole = lax.cond(segment == last, first, gather_rows)
    x_rows, slope, act, hidden, hg = saved

    def dispatch(grad):
        (send,) = call(place_body, [((n_expert, n_fsdp, 8, half), BF)], put, grad)
        return exchange(send)

    near_shape = ((n_fsdp, near_rows, hid), BF)

    near_slope, near_act, near_hid = lax.cond(
        segment == 1,
        lambda p, w: tuple(by_block(near_forward_body, [near_shape] * 3, [w], [p], first=2)),
        lambda *_: tuple(unfilled(near_shape, near_shape, near_shape)),
        plane,
        whole,
    )

    def exchange_near(value):
        cols = value.shape[-1]
        moved = lax.all_to_all(value.reshape(n_expert, 8, cols), "expert", 0, 0, tiled=True)
        return moved.reshape(near_rows, cols)

    gate_shape = ((1, micro, tok, top), F32)

    def relay(grad, new):
        (send,) = call(near_place_body, [((near_rows, half), BF)], put, grad)
        g_near = exchange_near(send)
        (out,) = by_block(
            near_back_body,
            [((near_rows, wide), BF)],
            [near_slope, near_act, near_hid, whole],
            [g_near],
            [(near_rows, half), (near_rows, half), (near_rows, LANES)],
        )
        back = exchange_near(out)
        new, gate = call(
            merge_gate_body, [((tokens, width), BF), gate_shape], near_get, near_getz, back, grad
        )
        return new, g_near, gate

    def relay_not(grad, new):
        return (new, *unfilled(((near_rows, half), BF), gate_shape))

    def middle(grad, state):
        g_rows = dispatch(grad)
        out, da, db, z = call_rows(
            back_body, rows_of(half, hid, hid, LANES), [g_rows, slope, act, hidden], [wd, wg, wu]
        )
        new = merge(exchange(out), grad)
        return new, z, g_rows, da, db

    def final(grad, state, done):
        g_rows = dispatch(grad)
        out, da, db = call_rows(
            back_body, rows_of(wide, hid, hid), [g_rows, slope, act, hidden], [wd, wg, wu]
        )
        back = exchange(out)
        grads = outer(x_rows, g_rows, da, db, hg)
        new, gate = call(
            merge_gate_body, [((tokens, width), BF), gate_shape], get, getz, back, grad
        )
        return (new, gate) + grads

    def collect(state, done):
        new, g_near, gate, _ = done
        g_all = jnp.zeros((n_expert, n_fsdp, 8, half), BF)
        for k, piece in enumerate(ring(g_near)):
            at = (0, (fsdp_now - k) % n_fsdp, 0, 0)
            g_all = lax.dynamic_update_slice(g_all, piece.reshape(n_expert, 1, 8, half), at)
        g_rows = g_all.reshape(total, half)
        da, db = call_rows(grad_body, rows_of(hid, hid), [g_rows, slope, act], [wd], SMALL)
        return gate, g_rows, da, db

    def settle(state, done):
        _, z, g_rows, da, db = state
        z = z + (0.0 * done[3][0]).astype(BF)
        return gate_of(exchange(z)), g_rows, da, db

    def finish(grad, state, done):
        gate, g_rows, da, db = lax.cond(segment == 1, collect, settle, state, done)
        return (done[0], gate) + outer(x_rows, g_rows, da, db, hg)

    def step_down(layer, new):
        return lax.ppermute(new, "segment", [(layer, layer - 1)])

    grad = step_down(last, state[0])
    for layer in range(last - 1, 1, -1):
        state = lax.cond(segment == layer, middle, lambda g, s: s, grad, state)
        grad = step_down(layer, state[0])
    new, g_near, gate = lax.cond(segment == 1, relay, relay_not, grad, state[0])
    grad = step_down(1, new)
    hold = lax.ppermute(1.0 + 0.0 * new[0, :8].astype(F32), "segment", [(1, last)])
    new, gate, grad_gate, grad_up, grad_down = lax.cond(
        segment == 0, final, finish, grad, state, (new, g_near, gate, hold)
    )
    return new.reshape(acts.shape), gate, grad_gate, grad_up, grad_down


def solution(mesh):
    in_specs = (
        P("segment", None, ("expert", "fsdp"), None),
        P(None, ("expert", "fsdp"), None),
        P("segment", None, ("expert", "fsdp"), None),
        P("segment", None, ("expert", "fsdp"), None),
        P("segment", "expert", None, "fsdp"),
        P("segment", "expert", None, "fsdp"),
        P("segment", "expert", "fsdp", None),
    )
    out_specs = (
        P("segment", None, ("expert", "fsdp"), None),
        P("segment", None, ("expert", "fsdp"), None),
        P("segment", "expert", None, "fsdp"),
        P("segment", "expert", None, "fsdp"),
        P("segment", "expert", "fsdp", None),
    )
    return jax.shard_map(local, mesh=mesh, in_specs=in_specs, out_specs=out_specs, check_vma=False)
```
